128 devices in a mesh: ctx: 16 (over y, z_lo, core), dp: 8 (over z_hi, x).
Axes of the slice: x: 4, y: 4, z: 4 (z_hi: 2, z_lo: 2; z = z_hi * 2 + z_lo), core: 2. Of those that a mesh axis runs over, the one named last changes fastest.
Arguments:
- query_rows: bfloat16 [8, 2048, 1024], P('dp', 'ctx'), may hold values from -6 to 6
- key_rows: bfloat16 [8, 2048, 1024], P('dp', 'ctx'), may hold values from -6 to 6
- value_rows: bfloat16 [8, 2048, 1024], P('dp', 'ctx'), may hold values from -6 to 6
- block_lists: int32 [8, 16, 4], P('dp'), may hold values from 0 to 15, as said below
- block_lengths: int32 [8, 16], P('dp'), may hold values from 2 to 128, as said below
- out_weight: bfloat16 [1024, 2048], replicated, may hold values from -0.125 to 0.125
- expert_input: bfloat16 [8, 2048, 2048], P('dp', 'ctx'), may hold values from -6 to 6
- layer_grad: bfloat16 [8, 2048, 2048], P('dp', 'ctx'), may hold values from -1.5 to 1.5
- route_experts: int32 [8, 2048, 6], P('dp', 'ctx'), may hold values from 0 to 15, all different within a row; in each aligned block of 128 rows (0 to 127, 128 to 255, ..., all dimensions but the last counted through in order) at most 64 rows name the same one
- route_weight: float32 [8, 2048, 6], P('dp', 'ctx'), may hold values from 0.02 to 0.4
- gate_weight: bfloat16 [16, 2048, 704], P('ctx'), may hold values from -0.125 to 0.125
- up_weight: bfloat16 [16, 2048, 704], P('ctx'), may hold values from -0.125 to 0.125
- down_weight: bfloat16 [16, 2048, 704], P('ctx'), may hold values from -0.21875 to 0.21875
Outputs:
- query_grad: bfloat16 [8, 2048, 1024], P('dp', 'ctx')
- key_grad: bfloat16 [8, 2048, 1024], P('dp', 'ctx')
- value_grad: bfloat16 [8, 2048, 1024], P('dp', 'ctx')
- gate_grad: float32 [16, 2048, 704], P('ctx', 'dp')
- up_grad: float32 [16, 2048, 704], P('ctx', 'dp')
- down_grad: float32 [16, 2048, 704], P('ctx', 'dp')
The draws below stay inside these ranges and needn't reach their ends.
Inputs may be any that keep to these rules, and one draw needn't show every extreme that they name: `block_lists`: entry 0 of row i of a sequence's lists is i; every entry of row i lies in 0 to i. `block_lengths`: every sequence has a block of full length 128. `route_experts`: each token names 6 different experts. Among the 128 tokens of one device, no expert is named by more than 64 tokens.
All inputs are finite; a program needn't handle non-finite values.
Results may differ from the reference program's by a relative error of at most 0.012.
The reference program's roundings to bfloat16 on the way count: a program that leaves them out, or rounds other values in their place, can miss the bound.
Values may be sent and summed in bfloat16 or wider, within the bound.
No kernel may reach another device: no remote copies, remote signals or barrier semaphores. Data moves between devices by JAX's collectives and lax.ppermute only.
A program may use at most 192 MiB of HBM per device.

```python
import math
from functools import partial
import jax
import jax.numpy as jnp
import numpy as np
from jax import lax

D = 2048
HEADS = 8
HD = 128
FFE = 704
TOPK = 6
BLK = 128
NSEL = 4
S_DEV = 128
SEQS = 8
LEN = 2048
NBLK = 16
EXPERTS = 16
CAP = 64
N_CTX = 16


def query_key_pair(key):
    base_key = jax.random.fold_in(key, 11)
    array_shape = (SEQS, LEN, HEADS * HD)
    queries = jax.random.truncated_normal(jax.random.fold_in(base_key, 1), -6.0, 6.0, array_shape, jnp.float32)
    keys_drawn = jax.random.truncated_normal(jax.random.fold_in(base_key, 2), -6.0, 6.0, array_shape, jnp.float32)
    return (queries, keys_drawn)


def draw_query_rows(key, part):
    return query_key_pair(key)[0].astype(jnp.bfloat16)


def draw_key_rows(key, part):
    return query_key_pair(key)[1].astype(jnp.bfloat16)


def draw_block_lists(key, part):
    block_rows = jnp.arange(NBLK, dtype=jnp.int32)
    upper_bound = jnp.broadcast_to((block_rows + 1)[None, :, None], (SEQS, NBLK, NSEL - 1))
    extra_blocks = jax.random.randint(jax.random.fold_in(key, 21), (SEQS, NBLK, NSEL - 1), 0, upper_bound, dtype=jnp.int32)
    diagonal = jnp.broadcast_to(block_rows[None, :, None], (SEQS, NBLK, 1))
    return jnp.concatenate([diagonal, extra_blocks], axis=2).astype(jnp.int32)


def draw_block_lengths(key, part):
    lengths = jax.random.randint(jax.random.fold_in(key, 31), (SEQS, NBLK), 2, BLK + 1, dtype=jnp.int32)
    full_block = jax.random.randint(jax.random.fold_in(key, 32), (SEQS, 1), 0, NBLK, dtype=jnp.int32)
    is_full = jnp.arange(NBLK, dtype=jnp.int32)[None, :] == full_block
    return jnp.where(is_full, BLK, lengths).astype(jnp.int32)


def block_levels(key, shape, cuts, least, largest):
    def one(position, shards_of):
        draws = jax.random.uniform(jax.random.fold_in(jax.random.fold_in(key, 6), position), (shards_of,), jnp.float32, least / len(cuts), largest / len(cuts))
        return jnp.repeat(jnp.exp(draws), shape[position] // shards_of).reshape((-1,) + (1,) * (len(shape) - position - 1))

    gain = one(*cuts[0])
    for cut in cuts[1:]:
        gain = gain * one(*cut)
    return gain


def deal_out(stream_key, own, number, rows, amount, top, limit, skew):
    order = jax.random.permutation(stream_key, amount)
    packed, ordinary = portions_of(amount, rows * top, limit, skew, True), portions_of(amount, rows * top, limit, skew, False)
    places = jnp.arange(amount)

    def named(sizes, rotation):
        used = int((sizes > 0).sum())
        fixed = max(1, used // 4)
        passed = fixed + (places - fixed + rotation * (used - fixed)) % max(1, amount - fixed)
        return jnp.zeros((amount,), jnp.int32).at[order[jnp.where(places < fixed, places, passed)]].set(jnp.asarray(sizes, jnp.int32))

    sizes = jnp.where(number % 4 == 0, named(packed, number // 4), named(ordinary, number - number // 4 - 1))
    mixed = jax.random.permutation(jax.random.fold_in(own, 3), amount)
    donor, sink = mixed[0:amount // 2 * 2:2], mixed[1:amount // 2 * 2:2]
    margin = jnp.minimum(sizes[donor] - 1, limit - sizes[sink]) // 2
    margin = jnp.where((donor == order[0]) | (sink == order[0]) | (sizes[sink] == 0), 0, jnp.maximum(margin, 0))
    passed = jax.random.randint(jax.random.fold_in(own, 4), (amount // 2,), 0, 1 << 20) % (margin + 1)
    sizes = sizes.at[donor].add(-passed).at[sink].add(passed)
    items = jnp.searchsorted(jnp.cumsum(sizes), jnp.arange(rows * top), side="right").astype(jnp.int32)
    grid = items.reshape(top, rows).T
    grid = grid[jax.random.permutation(jax.random.fold_in(own, 1), rows)]
    rotation = jax.random.randint(jax.random.fold_in(own, 2), (rows, 1), 0, top)
    return jnp.take_along_axis(grid, (jnp.arange(top)[None, :] + rotation) % top, axis=1)


def portions_of(number_of, total, most, lean, full):
    portions = [(1 << 20) // math.isqrt(standing ** lean) + 1 for standing in range(1, number_of + 1)]
    largest = most if full else min(most, max(-(-total // number_of), total * portions[0] // sum(portions)))
    least = 1 if total - largest >= number_of - 1 else 0
    counts, rest = [largest] + [least] * (number_of - 1), total - largest - least * (number_of - 1)
    while rest > 0:
        free = [i for i in range(1, number_of) if counts[i] < largest] or [i for i in range(1, number_of) if counts[i] < most]
        pool, left = sum([portions[i] for i in free]), rest
        for i in free:
            extra = min(most - counts[i], max(1, left * portions[i] // pool), rest)
            counts[i] = counts[i] + extra
            rest = rest - extra
    return np.array(counts)


def scatter_about(own_key, shape, scale, bound, shards=(), kind=jnp.bfloat16):
    level = block_levels(own_key, shape, shards, -0.22, 0.18) if shards else 1.0
    entries = jax.random.normal(own_key, shape, jnp.float32) * scale * level
    return jnp.minimum(jnp.maximum(entries, -bound), bound).astype(kind)


def setup_inputs(seed: int = 0) -> dict:
    arg_keys = jax.random.split(jax.random.key(seed), 14)
    query_rows = draw_query_rows(jax.random.fold_in(arg_keys[13], 71), 0)
    key_rows = draw_key_rows(jax.random.fold_in(arg_keys[13], 71), 0)
    value_rows = scatter_about(arg_keys[2], (SEQS, LEN, HEADS * HD), 1.0, 6.0, ((0, 8), (1, 16)))
    block_lists = draw_block_lists(jax.random.fold_in(arg_keys[13], 71), 0)
    block_lengths = draw_block_lengths(jax.random.fold_in(arg_keys[13], 71), 0)
    out_weight = scatter_about(arg_keys[5], (HEADS * HD, D), D ** -0.5, 0.125)
    expert_input = scatter_about(arg_keys[6], (SEQS, LEN, D), 1.0, 6.0, ((0, 8), (1, 16)))
    layer_grad = scatter_about(arg_keys[7], (SEQS, LEN, D), 0.25, 1.5, ((0, 8), (1, 16)))
    route_experts_keys = jax.random.split(jax.random.fold_in(arg_keys[8], 1), SEQS * LEN // S_DEV)
    route_experts_turns = jax.random.permutation(jax.random.fold_in(arg_keys[8], 3), SEQS * LEN // S_DEV)
    route_experts = jax.vmap(lambda own, number: deal_out(jax.random.fold_in(arg_keys[8], 2), own, number, S_DEV, EXPERTS, TOPK, CAP, 2))(route_experts_keys, route_experts_turns).reshape((SEQS, LEN, TOPK))
    route_weight = jnp.clip(jnp.exp(math.log(0.4) - 2.9957323 * jax.random.uniform(arg_keys[9], (SEQS, LEN, TOPK), jnp.float32) ** block_levels(arg_keys[9], (SEQS, LEN, TOPK), ((0, 8), (1, 16)), -0.2, 0.2)), 0.02, 0.4)
    gate_weight = scatter_about(arg_keys[10], (EXPERTS, D, FFE), D ** -0.5, 0.125, ((0, 16),))
    up_weight = scatter_about(arg_keys[11], (EXPERTS, D, FFE), D ** -0.5, 0.125, ((0, 16),))
    down_weight = scatter_about(arg_keys[12], (EXPERTS, D, FFE), FFE ** -0.5, 0.21875, ((0, 16),))
    return {"query_rows": query_rows, "key_rows": key_rows, "value_rows": value_rows, "block_lists": block_lists, "block_lengths": block_lengths, "out_weight": out_weight, "expert_input": expert_input, "layer_grad": layer_grad, "route_experts": route_experts, "route_weight": route_weight, "gate_weight": gate_weight, "up_weight": up_weight, "down_weight": down_weight}


def build_table(lists_row):
    numbers = jnp.arange(NBLK, dtype=jnp.int32)
    return jnp.any(lists_row[:, :, None] == numbers[None, None, :], axis=1)

def block_mask(table_mask, lengths_row, query_start, query_count, key_start, key_count):
    first_query = jnp.asarray(query_start, jnp.int32) // BLK
    first_key = jnp.asarray(key_start, jnp.int32) // BLK
    tile_part = lax.dynamic_slice(table_mask, (first_query, first_key), (query_count // BLK, key_count // BLK))
    spread = jnp.broadcast_to(tile_part[:, None, :, None], (query_count // BLK, BLK, key_count // BLK, BLK)).reshape(query_count, key_count)
    lengths_part = lax.dynamic_slice_in_dim(lengths_row, first_key, key_count // BLK, 0)
    offsets = jnp.arange(BLK, dtype=jnp.int32)
    present = (offsets[None, :] < lengths_part[:, None]).reshape(key_count)
    query_pos = jnp.asarray(query_start, jnp.int32) + jnp.arange(query_count, dtype=jnp.int32)
    key_pos = jnp.asarray(key_start, jnp.int32) + jnp.arange(key_count, dtype=jnp.int32)
    return spread & present[None, :] & (query_pos[:, None] >= key_pos[None, :])

def round_low(values):
    return lax.optimization_barrier(values.astype(jnp.bfloat16)).astype(jnp.float32)

def attention_sequence(queries, keys_all, values_all, lists_row, lengths_row, grads_in, out_weight):
    inv_root = 1.0 / math.sqrt(HD)
    out_grad = jnp.dot(grads_in, out_weight.T, preferred_element_type=jnp.float32).astype(jnp.bfloat16)
    table_mask = build_table(lists_row)
    query_heads = queries.astype(jnp.float32).reshape(LEN, HEADS, HD)
    key_heads = keys_all.astype(jnp.float32).reshape(LEN, HEADS, HD)
    value_heads = values_all.astype(jnp.float32).reshape(LEN, HEADS, HD)
    grad_heads = out_grad.astype(jnp.float32).reshape(LEN, HEADS, HD)
    row_block = min(LEN, 512)
    row_steps = LEN // row_block

    def row_step(running, step_index):
        row_start = step_index * row_block
        query_part = lax.dynamic_slice_in_dim(query_heads, row_start, row_block, 0)
        grad_part = lax.dynamic_slice_in_dim(grad_heads, row_start, row_block, 0)
        allowed = block_mask(table_mask, lengths_row, row_start, row_block, 0, LEN)
        raw_scores = jnp.einsum('qhd,khd->hqk', query_part, key_heads) * inv_root
        scores = jnp.where(allowed[None], raw_scores, -jnp.inf)
        row_max = lax.optimization_barrier(jnp.max(scores, axis=2, keepdims=True))
        log_total = row_max + jnp.log(lax.optimization_barrier(jnp.sum(jnp.exp(scores - row_max), axis=2, keepdims=True)))
        prob_full = jnp.exp(scores - log_total)
        prob_low = round_low(prob_full)
        head_output = jnp.einsum('hqk,khd->hqd', prob_low, value_heads)
        row_delta = lax.optimization_barrier(jnp.sum(jnp.swapaxes(head_output, 0, 1) * grad_part, axis=2))
        prob_grad = jnp.einsum('qhd,khd->hqk', grad_part, value_heads)
        dscore = round_low(prob_full * (prob_grad - row_delta.T[:, :, None]))
        query_block = (jnp.einsum('hqk,khd->qhd', dscore, key_heads) * inv_root).astype(jnp.bfloat16)
        key_acc = running[0] + jnp.einsum('hqk,qhd->khd', dscore, query_part) * inv_root
        value_acc = running[1] + jnp.einsum('hqk,qhd->khd', prob_low, grad_part)
        return ((key_acc, value_acc), query_block)
    zero_rows = jnp.zeros((LEN, HEADS, HD), jnp.float32)
    (key_acc, value_acc), query_blocks = lax.scan(row_step, (zero_rows, zero_rows), jnp.arange(row_steps, dtype=jnp.int32))
    query_grad = query_blocks.reshape(LEN, HEADS * HD)
    key_grad = key_acc.reshape(LEN, HEADS * HD).astype(jnp.bfloat16)
    value_grad = value_acc.reshape(LEN, HEADS * HD).astype(jnp.bfloat16)
    return (query_grad, key_grad, value_grad)

def route_coefficients(chosen, rweights, expert_list):
    matches = chosen[:, :, None] == expert_list[None, None, :]
    return lax.optimization_barrier(jnp.sum(jnp.where(matches, rweights[:, :, None], 0.0), axis=1))

def slot_rows(tokens, grad_rows, coef_rows, capacity):
    present = coef_rows > 0.0
    rank_rows = jnp.cumsum(present.astype(jnp.int32), axis=0) - 1
    slot_ids = jnp.arange(capacity, dtype=jnp.int32)
    chosen_slot = present.T[:, None, :] & (rank_rows.T[:, None, :] == slot_ids[None, :, None])
    onehot = chosen_slot.astype(jnp.float32)
    picked = jnp.einsum('ecs,sd->ecd', onehot, tokens.astype(jnp.float32)).astype(jnp.bfloat16)
    picked_grad = jnp.einsum('ecs,sd->ecd', onehot, grad_rows.astype(jnp.float32))
    slot_coef = lax.optimization_barrier(jnp.sum(jnp.where(chosen_slot, coef_rows.T[:, None, :], 0.0), axis=2))
    scaled = (slot_coef[:, :, None] * picked_grad).astype(jnp.bfloat16)
    return (picked, scaled)

def reference(query_rows, key_rows, value_rows, block_lists, block_lengths, out_weight, expert_input, layer_grad, route_experts, route_weight, gate_weight, up_weight, down_weight):

    def one_sequence(seq_index):
        return attention_sequence(query_rows[seq_index], key_rows[seq_index], value_rows[seq_index], block_lists[seq_index], block_lengths[seq_index], layer_grad[seq_index], out_weight)
    query_grad, key_grad, value_grad = lax.map(one_sequence, jnp.arange(SEQS, dtype=jnp.int32))
    block_count = SEQS * N_CTX
    token_blocks = expert_input.reshape(block_count, S_DEV, D)
    grad_blocks = layer_grad.reshape(block_count, S_DEV, D)
    chosen_blocks = route_experts.reshape(block_count, S_DEV, TOPK)
    weight_blocks = route_weight.reshape(block_count, S_DEV, TOPK)

    def one_expert(expert):
        expert_list = jnp.reshape(expert, (1,)).astype(jnp.int32)
        coef_all = jax.vmap(route_coefficients, in_axes=(0, 0, None))(chosen_blocks, weight_blocks, expert_list)
        picked, scaled = jax.vmap(partial(slot_rows, capacity=CAP))(token_blocks, grad_blocks, coef_all)
        rows_in = picked.reshape(SEQS, N_CTX * CAP, D).astype(jnp.float32)
        grads_in = scaled.reshape(SEQS, N_CTX * CAP, D).astype(jnp.float32)
        gate_pre = jnp.einsum('srd,df->srf', rows_in, gate_weight[expert].astype(jnp.float32))
        up_pre = jnp.einsum('srd,df->srf', rows_in, up_weight[expert].astype(jnp.float32))
        gate_sig = jax.nn.sigmoid(gate_pre)
        gate_act = gate_pre * gate_sig
        hidden = round_low(gate_act * up_pre)
        down_part = jnp.einsum('srd,srf->sdf', grads_in, hidden).astype(jnp.bfloat16)
        hidden_grad = jnp.einsum('srd,df->srf', grads_in, down_weight[expert].astype(jnp.float32))
        gate_delta = round_low(hidden_grad * up_pre * gate_sig * (1.0 + gate_pre * (1.0 - gate_sig)))
        up_delta = round_low(hidden_grad * gate_act)
        gate_part = jnp.einsum('srd,srf->sdf', rows_in, gate_delta).astype(jnp.bfloat16)
        up_part = jnp.einsum('srd,srf->sdf', rows_in, up_delta).astype(jnp.bfloat16)
        return (lax.optimization_barrier(jnp.sum(gate_part.astype(jnp.float32), axis=0)), lax.optimization_barrier(jnp.sum(up_part.astype(jnp.float32), axis=0)), lax.optimization_barrier(jnp.sum(down_part.astype(jnp.float32), axis=0)))
    gate_grad, up_grad, down_grad = lax.map(one_expert, jnp.arange(EXPERTS, dtype=jnp.int32))
    return (query_grad, key_grad, value_grad, gate_grad, up_grad, down_grad)
```

```python
import math

import jax
import jax.numpy as jnp
from jax import lax
from jax.experimental import pallas as pl
from jax.experimental.pallas import tpu as pltpu
from jax.sharding import PartitionSpec as P

HEADS = 8
HD = 128
TOPK = 6
BLK = 128
NSEL = 4
HALF = BLK // 2


def dot_nt(a, b):
    return lax.dot_general(a, b, (((1,), (1,)), ((), ())), preferred_element_type=jnp.float32)


def dot_nn(a, b):
    return lax.dot_general(a, b, (((1,), (0,)), ((), ())), preferred_element_type=jnp.float32)


def dot_tn(a, b):
    return lax.dot_general(a, b, (((0,), (0,)), ((), ())), preferred_element_type=jnp.float32)


def pack_kernel(q_ref, k_ref, v_ref, g_ref, w_ref, out_ref):
    out_grad = dot_nt(g_ref[...], w_ref[...]).astype(jnp.bfloat16)
    for half in range(2):
        rows = slice(half * HALF, (half + 1) * HALF)
        out_ref[half, 0:BLK, :] = k_ref[...]
        out_ref[half, BLK : 2 * BLK, :] = v_ref[...]
        out_ref[half, 2 * BLK : 2 * BLK + HALF, :] = q_ref[rows, :]
        out_ref[half, 2 * BLK + HALF :, :] = out_grad[rows, :]


def pack_rows(queries, keys, values, grads, out_weight):
    width = out_weight.shape[1]
    col = pl.BlockSpec((BLK, HD), lambda h: (0, h))
    return pl.pallas_call(
        pack_kernel,
        grid=(HEADS,),
        in_specs=[
            col,
            col,
            col,
            pl.BlockSpec((BLK, width), lambda h: (0, 0)),
            pl.BlockSpec((HD, width), lambda h: (h, 0)),
        ],
        out_specs=pl.BlockSpec((2, 3 * BLK, HD), lambda h: (h, 0, 0)),
        out_shape=jax.ShapeDtypeStruct((2 * HEADS, 3 * BLK, HD), jnp.bfloat16),
        cost_estimate=pl.CostEstimate(
            flops=2 * BLK * HEADS * HD * width, bytes_accessed=7_000_000, transcendentals=0
        ),
        name="pack_rows",
    )(queries, keys, values, grads, out_weight)


def attention_kernel(lists_ref, lengths_ref, half_ref, rows_ref, out_ref, key_acc, value_acc):
    inv_root = 1.0 / math.sqrt(HD)
    blocks = rows_ref.shape[0]
    key_acc[...] = jnp.zeros_like(key_acc)
    value_acc[...] = jnp.zeros_like(value_acc)
    query_at = lax.broadcasted_iota(jnp.int32, (HALF, BLK), 0) + half_ref[0] * HALF
    key_at = lax.broadcasted_iota(jnp.int32, (HALF, BLK), 1)

    def one_block(i, carry):
        query = rows_ref[i, 2 * BLK : 2 * BLK + HALF, :]
        grad = rows_ref[i, 2 * BLK + HALF :, :]
        listed = [lists_ref[i * NSEL + n] for n in range(NSEL)]
        scores = []
        for n, block in enumerate(listed):
            limit = lengths_ref[block]
            for earlier in listed[:n]:
                limit = jnp.where(earlier == block, 0, limit)
            reach = jnp.where(block < i, BLK, 0)
            allowed = (key_at < limit) & (key_at <= query_at + reach)
            raw = dot_nt(query, rows_ref[block, 0:BLK, :]) * inv_root
            scores.append(jnp.where(allowed, raw, -jnp.inf))
        top = scores[0]
        for part in scores[1:]:
            top = jnp.maximum(top, part)
        row_max = jnp.max(top, axis=1, keepdims=True)
        total = jnp.exp(scores[0] - row_max)
        for part in scores[1:]:
            total = total + jnp.exp(part - row_max)
        log_total = row_max + jnp.log(jnp.sum(total, axis=1, keepdims=True))
        probs = [jnp.exp(part - log_total) for part in scores]
        lows = [prob.astype(jnp.bfloat16) for prob in probs]
        head = dot_nn(lows[0], rows_ref[listed[0], BLK : 2 * BLK, :])
        for n in range(1, NSEL):
            head = head + dot_nn(lows[n], rows_ref[listed[n], BLK : 2 * BLK, :])
        row_delta = jnp.sum(head * grad.astype(jnp.float32), axis=1, keepdims=True)
        query_sum = jnp.zeros((HALF, HD), jnp.float32)
        for n, block in enumerate(listed):
            prob_grad = dot_nt(grad, rows_ref[block, BLK : 2 * BLK, :])
            dscore = (probs[n] * (prob_grad - row_delta)).astype(jnp.bfloat16)
            query_sum = query_sum + dot_nn(dscore, rows_ref[block, 0:BLK, :])
            key_acc[block] += dot_tn(dscore, query)
            value_acc[block] += dot_tn(lows[n], grad)
        out_ref[i, 2 * BLK :, :] = (query_sum * inv_root).astype(jnp.bfloat16)
        return carry

    lax.fori_loop(0, blocks, one_block, 0)
    for i in range(blocks):
        out_ref[i, 0:BLK, :] = (key_acc[i] * inv_root).astype(jnp.bfloat16)
        out_ref[i, BLK : 2 * BLK, :] = value_acc[i].astype(jnp.bfloat16)


def attention_rows(lists, lengths, half, rows):
    blocks = rows.shape[0]
    smem = pl.BlockSpec(memory_space=pltpu.SMEM)
    vmem = pl.BlockSpec(memory_space=pltpu.VMEM)
    return pl.pallas_call(
        attention_kernel,
        in_specs=[smem, smem, smem, vmem],
        out_specs=vmem,
        out_shape=jax.ShapeDtypeStruct((blocks, 2 * BLK + HALF, HD), jnp.bfloat16),
        scratch_shapes=[
            pltpu.VMEM((blocks, BLK, HD), jnp.float32),
            pltpu.VMEM((blocks, BLK, HD), jnp.float32),
        ],
        cost_estimate=pl.CostEstimate(
            flops=12 * blocks * NSEL * HALF * BLK * HD,
            bytes_accessed=3_000_000,
            transcendentals=2 * blocks * NSEL * HALF * BLK,
        ),
        name="attention_rows",
    )(lists, lengths, half, rows)


def unpack_kernel(rows_ref, query_ref, key_ref, value_ref):
    for h in range(HEADS):
        cols = slice(h * HD, (h + 1) * HD)

        def both(rows):
            first = rows_ref[2 * h, rows, :].astype(jnp.float32)
            return (first + rows_ref[2 * h + 1, rows, :].astype(jnp.float32)).astype(jnp.bfloat16)

        key_ref[:, cols] = both(slice(0, BLK))
        value_ref[:, cols] = both(slice(BLK, 2 * BLK))
        query_ref[0:HALF, cols] = rows_ref[2 * h, 2 * BLK :, :]
        query_ref[HALF:BLK, cols] = rows_ref[2 * h + 1, 2 * BLK :, :]


def unpack_rows(rows):
    vmem = pl.BlockSpec(memory_space=pltpu.VMEM)
    shape = jax.ShapeDtypeStruct((BLK, HEADS * HD), jnp.bfloat16)
    return pl.pallas_call(
        unpack_kernel,
        in_specs=[vmem],
        out_specs=(vmem, vmem, vmem),
        out_shape=(shape, shape, shape),
        cost_estimate=pl.CostEstimate(flops=0, bytes_accessed=2_000_000, transcendentals=0),
        name="unpack_rows",
    )(rows)


def route_coefficients(chosen, rweights, expert_list):
    matches = chosen[:, :, None] == expert_list[None, None, :]
    return jnp.sum(jnp.where(matches, rweights[:, :, None], 0.0), axis=1)


def slot_rows(tokens, grad_rows, coef_rows, capacity):
    present = coef_rows > 0.0
    rank_rows = jnp.cumsum(present.astype(jnp.int32), axis=0) - 1
    slot_ids = jnp.arange(capacity, dtype=jnp.int32)
    chosen_slot = present.T[:, None, :] & (rank_rows.T[:, None, :] == slot_ids[None, :, None])
    onehot = chosen_slot.astype(jnp.bfloat16)
    picked = jnp.einsum("ecs,sd->ecd", onehot, tokens, preferred_element_type=jnp.float32).astype(
        jnp.bfloat16
    )
    picked_grad = jnp.einsum("ecs,sd->ecd", onehot, grad_rows, preferred_element_type=jnp.float32)
    slot_coef = jnp.sum(jnp.where(chosen_slot, coef_rows.T[:, None, :], 0.0), axis=2)
    scaled = (slot_coef[:, :, None] * picked_grad).astype(jnp.bfloat16)
    return (picked, scaled)


def sum_over_sequences(part):
    count = lax.axis_size("dp")
    rows, columns = part.shape
    pieces = part.astype(jnp.bfloat16).reshape(count, rows // count, columns)
    arrived = lax.all_to_all(pieces, "dp", split_axis=0, concat_axis=0, tiled=True)
    return jnp.sum(arrived.astype(jnp.float32), axis=0)[None]


def per_device(
    query_rows,
    key_rows,
    value_rows,
    block_lists,
    block_lengths,
    out_weight,
    expert_input,
    layer_grad,
    route_experts,
    route_weight,
    gate_weight,
    up_weight,
    down_weight,
):
    ctx_count = lax.axis_size("ctx")
    my_index = lax.axis_index("ctx")
    tokens_here = expert_input[0]
    grads_here = layer_grad[0]
    capacity = min(BLK, BLK * TOPK * 4 // (3 * ctx_count))
    all_experts = jnp.arange(ctx_count, dtype=jnp.int32)
    coef_here = route_coefficients(route_experts[0], route_weight[0], all_experts)
    picked, scaled = slot_rows(tokens_here, grads_here, coef_here, capacity)
    rows_in = lax.all_to_all(picked, "ctx", split_axis=0, concat_axis=0, tiled=True)
    grads_in = lax.all_to_all(scaled, "ctx", split_axis=0, concat_axis=0, tiled=True)
    packed = pack_rows(query_rows[0], key_rows[0], value_rows[0], grads_here, out_weight)
    packed, grads_in = lax.optimization_barrier((packed, grads_in))
    rows_in = rows_in.reshape(ctx_count * capacity, -1)
    grads_in = grads_in.reshape(ctx_count * capacity, -1)
    head_rows = lax.all_to_all(packed, "ctx", split_axis=0, concat_axis=0, tiled=True)

    gate_pre = dot_nn(rows_in, gate_weight[0])
    up_pre = dot_nn(rows_in, up_weight[0])
    gate_sig = jax.nn.sigmoid(gate_pre)
    gate_act = gate_pre * gate_sig
    hidden = (gate_act * up_pre).astype(jnp.bfloat16)
    down_part = dot_tn(grads_in, hidden)
    down_grad = sum_over_sequences(down_part)
    hidden_grad = dot_nn(grads_in, down_weight[0])
    gate_delta = (hidden_grad * up_pre * gate_sig * (1.0 + gate_pre * (1.0 - gate_sig))).astype(
        jnp.bfloat16
    )
    up_delta = (hidden_grad * gate_act).astype(jnp.bfloat16)
    gate_part = dot_tn(rows_in, gate_delta)
    gate_grad = sum_over_sequences(gate_part)
    up_part = dot_tn(rows_in, up_delta)
    up_grad = sum_over_sequences(up_part)

    half = (my_index % 2).astype(jnp.int32).reshape(1)
    grad_rows = attention_rows(
        block_lists.reshape(-1), block_lengths.reshape(-1), half, head_rows
    )
    returned = lax.all_to_all(grad_rows, "ctx", split_axis=0, concat_axis=0, tiled=True)
    query_grad, key_grad, value_grad = unpack_rows(returned)
    return (query_grad[None], key_grad[None], value_grad[None], gate_grad, up_grad, down_grad)


def solution(mesh):
    in_specs = (
        P("dp", "ctx", None),
        P("dp", "ctx", None),
        P("dp", "ctx", None),
        P("dp", None, None),
        P("dp", None),
        P(),
        P("dp", "ctx", None),
        P("dp", "ctx", None),
        P("dp", "ctx", None),
        P("dp", "ctx", None),
        P("ctx", None, None),
        P("ctx", None, None),
        P("ctx", None, None),
    )
    out_specs = (
        P("dp", "ctx", None),
        P("dp", "ctx", None),
        P("dp", "ctx", None),
        P("ctx", "dp", None),
        P("ctx", "dp", None),
        P("ctx", "dp", None),
    )
    return jax.shard_map(
        per_device, mesh=mesh, in_specs=in_specs, out_specs=out_specs, check_vma=False
    )
```

```python
import math

import jax
import jax.numpy as jnp
from jax import lax
from jax.experimental import pallas as pl
from jax.experimental.pallas import tpu as pltpu
from jax.sharding import PartitionSpec as P

HEADS = 8
HD = 128
TOPK = 6
BLK = 128
NSEL = 4
HALF = BLK // 2


def dot_nt(a, b):
    return lax.dot_general(a, b, (((1,), (1,)), ((), ())), preferred_element_type=jnp.float32)


def dot_nn(a, b):
    return lax.dot_general(a, b, (((1,), (0,)), ((), ())), preferred_element_type=jnp.float32)


def dot_tn(a, b):
    return lax.dot_general(a, b, (((0,), (0,)), ((), ())), preferred_element_type=jnp.float32)


def pack_kernel(q_ref, k_ref, v_ref, g_ref, w_ref, out_ref):
    out_grad = dot_nt(g_ref[...], w_ref[...]).astype(jnp.bfloat16)
    for half in range(2):
        rows = slice(half * HALF, (half + 1) * HALF)
        out_ref[half, 0:BLK, :] = k_ref[...]
        out_ref[half, BLK : 2 * BLK, :] = v_ref[...]
        out_ref[half, 2 * BLK : 2 * BLK + HALF, :] = q_ref[rows, :]
        out_ref[half, 2 * BLK + HALF :, :] = out_grad[rows, :]


def pack_rows(queries, keys, values, grads, out_weight):
    width = out_weight.shape[1]
    col = pl.BlockSpec((BLK, HD), lambda h: (0, h))
    return pl.pallas_call(
        pack_kernel,
        grid=(HEADS,),
        in_specs=[
            col,
            col,
            col,
            pl.BlockSpec((BLK, width), lambda h: (0, 0)),
            pl.BlockSpec((HD, width), lambda h: (h, 0)),
        ],
        out_specs=pl.BlockSpec((2, 3 * BLK, HD), lambda h: (h, 0, 0)),
        out_shape=jax.ShapeDtypeStruct((2 * HEADS, 3 * BLK, HD), jnp.bfloat16),
        cost_estimate=pl.CostEstimate(
            flops=2 * BLK * HEADS * HD * width, bytes_accessed=7_000_000, transcendentals=0
        ),
        name="pack_rows",
    )(queries, keys, values, grads, out_weight)


def attention_kernel(lists_ref, lengths_ref, half_ref, rows_ref, out_ref, key_acc, value_acc):
    inv_root = 1.0 / math.sqrt(HD)
    blocks = rows_ref.shape[0]
    key_acc[...] = jnp.zeros_like(key_acc)
    value_acc[...] = jnp.zeros_like(value_acc)
    query_at = lax.broadcasted_iota(jnp.int32, (HALF, BLK), 0) + half_ref[0] * HALF
    key_at = lax.broadcasted_iota(jnp.int32, (HALF, BLK), 1)

    def one_block(i, carry):
        query = rows_ref[i, 2 * BLK : 2 * BLK + HALF, :]
        grad = rows_ref[i, 2 * BLK + HALF :, :]
        listed = [lists_ref[i * NSEL + n] for n in range(NSEL)]
        scores = []
        for n, block in enumerate(listed):
            limit = lengths_ref[block]
            for earlier in listed[:n]:
                limit = jnp.where(earlier == block, 0, limit)
            reach = jnp.where(block < i, BLK, 0)
            allowed = (key_at < limit) & (key_at <= query_at + reach)
            raw = dot_nt(query, rows_ref[block, 0:BLK, :]) * inv_root
            scores.append(jnp.where(allowed, raw, -jnp.inf))
        top = scores[0]
        for part in scores[1:]:
            top = jnp.maximum(top, part)
        row_max = jnp.max(top, axis=1, keepdims=True)
        total = jnp.exp(scores[0] - row_max)
        for part in scores[1:]:
            total = total + jnp.exp(part - row_max)
        log_total = row_max + jnp.log(jnp.sum(total, axis=1, keepdims=True))
        probs = [jnp.exp(part - log_total) for part in scores]
        lows = [prob.astype(jnp.bfloat16) for prob in probs]
        head = dot_nn(lows[0], rows_ref[listed[0], BLK : 2 * BLK, :])
        for n in range(1, NSEL):
            head = head + dot_nn(lows[n], rows_ref[listed[n], BLK : 2 * BLK, :])
        row_delta = jnp.sum(head * grad.astype(jnp.float32), axis=1, keepdims=True)
        query_sum = jnp.zeros((HALF, HD), jnp.float32)
        for n, block in enumerate(listed):
            prob_grad = dot_nt(grad, rows_ref[block, BLK : 2 * BLK, :])
            dscore = (probs[n] * (prob_grad - row_delta)).astype(jnp.bfloat16)
            query_sum = query_sum + dot_nn(dscore, rows_ref[block, 0:BLK, :])
            key_acc[block] += dot_tn(dscore, query)
            value_acc[block] += dot_tn(lows[n], grad)
        out_ref[i, 2 * BLK :, :] = (query_sum * inv_root).astype(jnp.bfloat16)
        return carry

    lax.fori_loop(0, blocks, one_block, 0)
    for i in range(blocks):
        out_ref[i, 0:BLK, :] = (key_acc[i] * inv_root).astype(jnp.bfloat16)
        out_ref[i, BLK : 2 * BLK, :] = value_acc[i].astype(jnp.bfloat16)


def attention_rows(lists, lengths, half, rows):
    blocks = rows.shape[0]
    smem = pl.BlockSpec(memory_space=pltpu.SMEM)
    vmem = pl.BlockSpec(memory_space=pltpu.VMEM)
    return pl.pallas_call(
        attention_kernel,
        in_specs=[smem, smem, smem, vmem],
        out_specs=vmem,
        out_shape=jax.ShapeDtypeStruct((blocks, 2 * BLK + HALF, HD), jnp.bfloat16),
        scratch_shapes=[
            pltpu.VMEM((blocks, BLK, HD), jnp.float32),
            pltpu.VMEM((blocks, BLK, HD), jnp.float32),
        ],
        cost_estimate=pl.CostEstimate(
            flops=12 * blocks * NSEL * HALF * BLK * HD,
            bytes_accessed=3_000_000,
            transcendentals=2 * blocks * NSEL * HALF * BLK,
        ),
        name="attention_rows",
    )(lists, lengths, half, rows)


def unpack_kernel(rows_ref, query_ref, key_ref, value_ref):
    for h in range(HEADS):
        cols = slice(h * HD, (h + 1) * HD)

        def both(rows):
            first = rows_ref[2 * h, rows, :].astype(jnp.float32)
            return (first + rows_ref[2 * h + 1, rows, :].astype(jnp.float32)).astype(jnp.bfloat16)

        key_ref[:, cols] = both(slice(0, BLK))
        value_ref[:, cols] = both(slice(BLK, 2 * BLK))
        query_ref[0:HALF, cols] = rows_ref[2 * h, 2 * BLK :, :]
        query_ref[HALF:BLK, cols] = rows_ref[2 * h + 1, 2 * BLK :, :]


def unpack_rows(rows):
    vmem = pl.BlockSpec(memory_space=pltpu.VMEM)
    shape = jax.ShapeDtypeStruct((BLK, HEADS * HD), jnp.bfloat16)
    return pl.pallas_call(
        unpack_kernel,
        in_specs=[vmem],
        out_specs=(vmem, vmem, vmem),
        out_shape=(shape, shape, shape),
        cost_estimate=pl.CostEstimate(flops=0, bytes_accessed=2_000_000, transcendentals=0),
        name="unpack_rows",
    )(rows)


def chip_moves(move):
    def index(y, z, core):
        return (y % 4) * 4 + (z % 2) * 2 + core % 2

    return [
        (index(y, z, core), index(*move(y, z, core)))
        for y in range(4)
        for z in range(2)
        for core in range(2)
    ]


Y_UP = chip_moves(lambda y, z, core: (y + 1, z, core))
Y_DOWN = chip_moves(lambda y, z, core: (y - 1, z, core))
Z_SWAP = chip_moves(lambda y, z, core: (y, z + 1, core))
CORE_SWAP = chip_moves(lambda y, z, core: (y, z, core + 1))
PIECE_STEPS = ((0, 0), (0, 1), (-1, 0), (1, 0), (-1, 1), (1, 1), (-2, 0), (2, 1))
LATE = 2


def sequence_moves(move):
    def index(z, x):
        return (z % 2) * 4 + x % 4

    return [(index(z, x), index(*move(z, x))) for z in range(2) for x in range(4)]


X_UP = sequence_moves(lambda z, x: (z, x + 1))
X_DOWN = sequence_moves(lambda z, x: (z, x - 1))
FAR_SWAP = sequence_moves(lambda z, x: (z + 1, x))


def after(value, *others):
    return lax.optimization_barrier((value, *others))[0]


def collect_pieces(own, side_gate, ring_gate):
    to_side = after(own, *side_gate)
    to_ring = after(own, *ring_gate)
    beside = lax.ppermute(to_side, "ctx", Z_SWAP)
    below = lax.ppermute(to_ring, "ctx", Y_UP)
    above = lax.ppermute(to_ring, "ctx", Y_DOWN)
    below_beside = lax.ppermute(beside, "ctx", Y_UP)
    above_beside = lax.ppermute(beside, "ctx", Y_DOWN)
    far = lax.ppermute(below, "ctx", Y_UP)
    far_beside = lax.ppermute(above_beside, "ctx", Y_DOWN)
    mine = [own, beside, below, above, below_beside, above_beside, far, far_beside]
    return mine, [lax.ppermute(piece, "ctx", CORE_SWAP) for piece in mine]


def piece_sources(my_index):
    y, z, core = my_index // 4, (my_index // 2) % 2, my_index % 2
    places = []
    for step in range(2):
        for dy, dz in PIECE_STEPS:
            places.append(((y + dy + 4) % 4) * 4 + ((z + dz) % 2) * 2 + (core + step) % 2)
    return jnp.stack(places)


def pick_kernel(count, scaled, *refs):
    onehot_ref, coef_ref = refs[0], refs[1]
    pieces, out_ref = refs[2 : 2 + count], refs[-1]
    slots = onehot_ref.shape[1]
    for p, piece in enumerate(pieces):
        picked = dot_nn(onehot_ref[p], piece[...])
        if scaled:
            picked = picked * coef_ref[p]
        out_ref[p * slots : (p + 1) * slots, :] = picked.astype(jnp.bfloat16)


def pick_rows(onehot, coef, pieces, scaled, buffer, first):
    count, (rows, width), slots = len(pieces), pieces[0].shape, onehot.shape[1]
    tile = 512
    total = 2 * len(PIECE_STEPS) * slots
    in_specs = [
        pl.BlockSpec((count, slots, rows), lambda j: (0, 0, 0)),
        pl.BlockSpec((count, slots, 1), lambda j: (0, 0, 0)),
    ] + [pl.BlockSpec((rows, tile), lambda j: (0, j))] * count
    operands = [onehot, coef, *pieces]
    aliases = {}
    if buffer is not None:
        aliases = {len(operands): 0}
        operands.append(buffer)
        in_specs.append(pl.BlockSpec(memory_space=pl.ANY))
    block = count * slots
    return pl.pallas_call(
        lambda *refs: pick_kernel(count, scaled, *refs),
        grid=(width // tile,),
        in_specs=in_specs,
        out_specs=pl.BlockSpec((block, tile), lambda j: (first // block, j)),
        out_shape=jax.ShapeDtypeStruct((total, width), jnp.bfloat16),
        input_output_aliases=aliases,
        cost_estimate=pl.CostEstimate(
            flops=2 * block * rows * width,
            bytes_accessed=2 * count * (rows + slots) * width,
            transcendentals=0,
        ),
        name="pick_rows",
    )(*operands)


def pick_all(onehot, coef, mine, others, scaled):
    early, keep = 2 * len(PIECE_STEPS) - 2 * LATE, len(PIECE_STEPS) - LATE
    buffer = pick_rows(
        onehot[:early], coef[:early], mine[:keep] + others[:keep], scaled, None, 0
    )
    first = early * onehot.shape[1]
    return pick_rows(onehot[early:], coef[early:], mine[keep:] + others[keep:], scaled, buffer, first)


def route_slots(coef_rows, capacity):
    present = coef_rows > 0.0
    rank = jnp.cumsum(present.astype(jnp.int32), axis=1) - 1
    slot_ids = jnp.arange(capacity, dtype=jnp.int32)
    chosen = present[:, None, :] & (rank[:, None, :] == slot_ids[None, :, None])
    slot_coef = jnp.sum(jnp.where(chosen, coef_rows[:, None, :], 0.0), axis=2, keepdims=True)
    return chosen.astype(jnp.bfloat16), slot_coef


def term_kernel(order_ref, delta_ref, rows_ref, *out_refs):
    step = pl.program_id(0)
    value = dot_nn(delta_ref[...], rows_ref[...]).astype(jnp.bfloat16)
    for t, out_ref in enumerate(out_refs):

        @pl.when(step == t)
        def _(out_ref=out_ref):
            out_ref[...] = value


def weight_terms(order, delta, rows):
    count = order.shape[0]
    hidden, slots = delta.shape
    tile = rows.shape[1] // count
    whole = pl.BlockSpec((hidden, tile), lambda j, order_ref: (0, 0))
    shape = jax.ShapeDtypeStruct((hidden, tile), jnp.bfloat16)
    return pl.pallas_call(
        term_kernel,
        grid_spec=pltpu.PrefetchScalarGridSpec(
            num_scalar_prefetch=1,
            grid=(count,),
            in_specs=[
                pl.BlockSpec((hidden, slots), lambda j, order_ref: (0, 0)),
                pl.BlockSpec((slots, tile), lambda j, order_ref: (0, order_ref[j])),
            ],
            out_specs=[whole] * count,
        ),
        out_shape=[shape] * count,
        cost_estimate=pl.CostEstimate(
            flops=2 * hidden * slots * count * tile, bytes_accessed=9_000_000, transcendentals=0
        ),
        name="weight_terms",
    )(order, delta, rows)


def term_order():
    place = lax.axis_index("dp")
    z, x = place // 4, place % 4
    steps = ((2, 0), (2, 1), (1, 1), (3, 0), (1, 0), (3, 1), (0, 1), (0, 0))
    return jnp.stack([((z + dz) % 2) * 4 + (x + dx) % 4 for dx, dz in steps]).astype(jnp.int32)


def add_terms(*terms):
    total = terms[0].astype(jnp.float32)
    for term in terms[1:]:
        total = total + term.astype(jnp.float32)
    return total


def sum_over_sequences(terms):
    far_same, far_other, next_other, back_same, next_same, back_other, own_other, own_same = terms
    up_far = lax.ppermute(far_same, "dp", X_UP)
    down_far = lax.ppermute(far_other, "dp", X_DOWN)
    up_other = lax.ppermute(next_other, "dp", X_UP)
    down_same = lax.ppermute(back_same, "dp", X_DOWN)
    send_down = add_terms(back_other, down_far).astype(jnp.bfloat16)
    down_other = lax.ppermute(send_down, "dp", X_DOWN)
    send_up = add_terms(next_same, up_far).astype(jnp.bfloat16)
    up_same = lax.ppermute(send_up, "dp", X_UP)
    across = add_terms(own_other, up_other, down_other).astype(jnp.bfloat16)
    arrived = lax.ppermute(across, "dp", FAR_SWAP)
    return add_terms(own_same, up_same, down_same, arrived).T[None]


def per_device(
    query_rows,
    key_rows,
    value_rows,
    block_lists,
    block_lengths,
    out_weight,
    expert_input,
    layer_grad,
    route_experts,
    route_weight,
    gate_weight,
    up_weight,
    down_weight,
):
    ctx_count = lax.axis_size("ctx")
    my_index = lax.axis_index("ctx")
    tokens_here = expert_input[0]
    grads_here = layer_grad[0]
    capacity = min(BLK, BLK * TOPK * 4 // (3 * ctx_count))

    all_experts = jnp.arange(ctx_count, dtype=jnp.int32)
    matches = route_experts[0][None, :, :] == all_experts[:, None, None]
    coef_out = jnp.sum(jnp.where(matches, route_weight[0][None], 0.0), axis=2)
    coef_in = lax.all_to_all(coef_out, "ctx", split_axis=0, concat_axis=0, tiled=True)
    onehot, slot_coef = route_slots(coef_in[piece_sources(my_index)], capacity)
    keep = len(PIECE_STEPS) - LATE
    halves = (slice(0, keep), slice(keep + LATE, 2 * keep + LATE))
    tails = (slice(keep, keep + LATE), slice(2 * keep + LATE, None))
    onehot, slot_coef = (
        jnp.concatenate([v[part] for part in halves + tails]) for v in (onehot, slot_coef)
    )

    mine, others = collect_pieces(tokens_here, (), ())
    grad_mine, grad_others = collect_pieces(grads_here, (mine[1],), (mine[4], mine[5]))
    rows_in = pick_all(onehot, slot_coef, mine, others, False)
    grads_in = pick_all(onehot, slot_coef, grad_mine, grad_others, True)

    packed = pack_rows(query_rows[0], key_rows[0], value_rows[0], grads_here, out_weight)
    packed = after(packed, grad_mine[-1], grad_mine[-2])
    head_rows = lax.all_to_all(packed, "ctx", split_axis=0, concat_axis=0, tiled=True)

    order = term_order()
    gate_pre = dot_nn(rows_in, gate_weight[0])
    up_pre = dot_nn(rows_in, up_weight[0])
    gate_sig = jax.nn.sigmoid(gate_pre)
    gate_act = gate_pre * gate_sig
    hidden = (gate_act * up_pre).astype(jnp.bfloat16)
    down_grad = sum_over_sequences(weight_terms(order, hidden.T, grads_in))
    hidden_grad = dot_nn(grads_in, down_weight[0])
    gate_delta = (hidden_grad * up_pre * gate_sig * (1.0 + gate_pre * (1.0 - gate_sig))).astype(
        jnp.bfloat16
    )
    up_delta = (hidden_grad * gate_act).astype(jnp.bfloat16)
    gate_grad = sum_over_sequences(weight_terms(order, gate_delta.T, rows_in))
    up_terms = weight_terms(order, up_delta.T, rows_in)
    up_grad = sum_over_sequences(up_terms)

    half = (my_index % 2).astype(jnp.int32).reshape(1)
    head_rows = after(head_rows, up_terms[0])
    grad_rows = attention_rows(
        block_lists.reshape(-1), block_lengths.reshape(-1), half, head_rows
    )
    returned = lax.all_to_all(grad_rows, "ctx", split_axis=0, concat_axis=0, tiled=True)
    query_grad, key_grad, value_grad = unpack_rows(returned)
    return (query_grad[None], key_grad[None], value_grad[None], gate_grad, up_grad, down_grad)


def solution(mesh):
    in_specs = (
        P("dp", "ctx", None),
        P("dp", "ctx", None),
        P("dp", "ctx", None),
        P("dp", None, None),
        P("dp", None),
        P(),
        P("dp", "ctx", None),
        P("dp", "ctx", None),
        P("dp", "ctx", None),
        P("dp", "ctx", None),
        P("ctx", None, None),
        P("ctx", None, None),
        P("ctx", None, None),
    )
    out_specs = (
        P("dp", "ctx", None),
        P("dp", "ctx", None),
        P("dp", "ctx", None),
        P("ctx", "dp", None),
        P("ctx", "dp", None),
        P("ctx", "dp", None),
    )
    return jax.shard_map(
        per_device, mesh=mesh, in_specs=in_specs, out_specs=out_specs, check_vma=False
    )
```

```python
import math

import jax
import jax.numpy as jnp
from jax import lax
from jax.experimental import pallas as pl
from jax.experimental.pallas import tpu as pltpu
from jax.sharding import PartitionSpec as P


HEADS = 8
HD = 128
TOPK = 6
BLK = 128
NSEL = 4
HALF = BLK // 2
TOGETHER = 2


def dot_nt(a, b):
    return lax.dot_general(a, b, (((1,), (1,)), ((), ())), preferred_element_type=jnp.float32)


def dot_nn(a, b):
    return lax.dot_general(a, b, (((1,), (0,)), ((), ())), preferred_element_type=jnp.float32)


def dot_tn(a, b):
    return lax.dot_general(a, b, (((0,), (0,)), ((), ())), preferred_element_type=jnp.float32)


def pack_kernel(q_ref, k_ref, v_ref, g_ref, w_ref, out_ref):
    out_grad = dot_nt(g_ref[...], w_ref[...]).astype(jnp.bfloat16)
    for head in range(2):
        cols = slice(head * HD, (head + 1) * HD)
        for half in range(2):
            rows, place = slice(half * HALF, (half + 1) * HALF), 2 * head + half
            out_ref[place, 0:BLK, :] = k_ref[:, cols]
            out_ref[place, BLK : 2 * BLK, :] = v_ref[:, cols]
            out_ref[place, 2 * BLK : 2 * BLK + HALF, :] = q_ref[rows, cols]
            out_ref[place, 2 * BLK + HALF :, :] = out_grad[rows, cols]


def pack_rows(queries, keys, values, grads, out_weight):
    width = out_weight.shape[1]
    col = pl.BlockSpec((BLK, 2 * HD), lambda h: (0, h))
    return pl.pallas_call(
        pack_kernel,
        grid=(HEADS // 2,),
        in_specs=[
            col,
            col,
            col,
            pl.BlockSpec((BLK, width), lambda h: (0, 0)),
            pl.BlockSpec((2 * HD, width), lambda h: (h, 0)),
        ],
        out_specs=pl.BlockSpec((4, 3 * BLK, HD), lambda h: (h, 0, 0)),
        out_shape=jax.ShapeDtypeStruct((2 * HEADS, 3 * BLK, HD), jnp.bfloat16),
        cost_estimate=pl.CostEstimate(
            flops=2 * BLK * HEADS * HD * width, bytes_accessed=7_000_000, transcendentals=0
        ),
        name="pack_rows",
    )(queries, keys, values, grads, out_weight)


def attention_kernel(lists_ref, lengths_ref, half_ref, rows_ref, out_ref, key_acc, value_acc):
    inv_root = 1.0 / math.sqrt(HD)
    blocks = rows_ref.shape[0]
    key_acc[...] = jnp.zeros_like(key_acc)
    value_acc[...] = jnp.zeros_like(value_acc)
    query_at = lax.broadcasted_iota(jnp.int32, (HALF, BLK), 0) + half_ref[0] * HALF
    key_at = lax.broadcasted_iota(jnp.int32, (HALF, BLK), 1)

    def score(i):
        query = rows_ref[i, 2 * BLK : 2 * BLK + HALF, :]
        listed = [lists_ref[i * NSEL + n] for n in range(NSEL)]
        scores = []
        for n, block in enumerate(listed):
            limit = lengths_ref[block]
            for earlier in listed[:n]:
                limit = jnp.where(earlier == block, 0, limit)
            reach = jnp.where(block < i, BLK, 0)
            allowed = (key_at < limit) & (key_at <= query_at + reach)
            raw = dot_nt(query, rows_ref[block, 0:BLK, :]) * inv_root
            scores.append(jnp.where(allowed, raw, -jnp.inf))
        return listed, scores

    def normalize(scores):
        top = scores[0]
        for part in scores[1:]:
            top = jnp.maximum(top, part)
        row_max = jnp.max(top, axis=1, keepdims=True)
        total = jnp.exp(scores[0] - row_max)
        for part in scores[1:]:
            total = total + jnp.exp(part - row_max)
        log_total = row_max + jnp.log(jnp.sum(total, axis=1, keepdims=True))
        return [jnp.exp(part - log_total) for part in scores]

    def terms(i, listed, probs):
        query = rows_ref[i, 2 * BLK : 2 * BLK + HALF, :]
        grad = rows_ref[i, 2 * BLK + HALF :, :]
        lows = [prob.astype(jnp.bfloat16) for prob in probs]
        head = dot_nn(lows[0], rows_ref[listed[0], BLK : 2 * BLK, :])
        for n in range(1, NSEL):
            head = head + dot_nn(lows[n], rows_ref[listed[n], BLK : 2 * BLK, :])
        prob_grads = [dot_nt(grad, rows_ref[block, BLK : 2 * BLK, :]) for block in listed]
        row_delta = jnp.sum(head * grad.astype(jnp.float32), axis=1, keepdims=True)
        dscores = [
            (prob * (prob_grad - row_delta)).astype(jnp.bfloat16)
            for prob, prob_grad in zip(probs, prob_grads)
        ]
        query_sum = dot_nn(dscores[0], rows_ref[listed[0], 0:BLK, :])
        for n in range(1, NSEL):
            query_sum = query_sum + dot_nn(dscores[n], rows_ref[listed[n], 0:BLK, :])
        key_terms = [dot_tn(dscore, query) for dscore in dscores]
        value_terms = [dot_tn(low, grad) for low in lows]
        return query_sum, key_terms, value_terms

    def some_blocks(group, carry):
        rows = [group * TOGETHER + u for u in range(TOGETHER)]
        scored = [score(i) for i in rows]
        probs = [normalize(scores) for _, scores in scored]
        results = [terms(i, scored[u][0], probs[u]) for u, i in enumerate(rows)]
        for u, i in enumerate(rows):
            query_sum, key_terms, value_terms = results[u]
            out_ref[i, 2 * BLK :, :] = (query_sum * inv_root).astype(jnp.bfloat16)
            for n, block in enumerate(scored[u][0]):
                key_acc[block] += key_terms[n]
                value_acc[block] += value_terms[n]
        return carry

    lax.fori_loop(0, blocks // TOGETHER, some_blocks, 0)
    for i in range(blocks):
        out_ref[i, 0:BLK, :] = (key_acc[i] * inv_root).astype(jnp.bfloat16)
        out_ref[i, BLK : 2 * BLK, :] = value_acc[i].astype(jnp.bfloat16)


def attention_rows(lists, lengths, half, rows):
    blocks = rows.shape[0]
    smem = pl.BlockSpec(memory_space=pltpu.SMEM)
    vmem = pl.BlockSpec(memory_space=pltpu.VMEM)
    return pl.pallas_call(
        attention_kernel,
        in_specs=[smem, smem, smem, vmem],
        out_specs=vmem,
        out_shape=jax.ShapeDtypeStruct((blocks, 2 * BLK + HALF, HD), jnp.bfloat16),
        scratch_shapes=[
            pltpu.VMEM((blocks, BLK, HD), jnp.float32),
            pltpu.VMEM((blocks, BLK, HD), jnp.float32),
        ],
        cost_estimate=pl.CostEstimate(flops=0, bytes_accessed=3_000_000, transcendentals=0),
        name="attention_rows",
    )(lists, lengths, half, rows)


def unpack_kernel(rows_ref, query_ref, key_ref, value_ref):
    for h in range(HEADS):
        cols = slice(h * HD, (h + 1) * HD)

        def both(rows):
            first = rows_ref[2 * h, rows, :].astype(jnp.float32)
            return (first + rows_ref[2 * h + 1, rows, :].astype(jnp.float32)).astype(jnp.bfloat16)

        key_ref[:, cols] = both(slice(0, BLK))
        value_ref[:, cols] = both(slice(BLK, 2 * BLK))
        query_ref[0:HALF, cols] = rows_ref[2 * h, 2 * BLK :, :]
        query_ref[HALF:BLK, cols] = rows_ref[2 * h + 1, 2 * BLK :, :]


def unpack_rows(rows):
    vmem = pl.BlockSpec(memory_space=pltpu.VMEM)
    shape = jax.ShapeDtypeStruct((BLK, HEADS * HD), jnp.bfloat16)
    return pl.pallas_call(
        unpack_kernel,
        in_specs=[vmem],
        out_specs=(vmem, vmem, vmem),
        out_shape=(shape, shape, shape),
        cost_estimate=pl.CostEstimate(flops=0, bytes_accessed=2_000_000, transcendentals=0),
        name="unpack_rows",
    )(rows)


def chip_moves(move):
    def index(y, z, core):
        return (y % 4) * 4 + (z % 2) * 2 + core % 2

    return [
        (index(y, z, core), index(*move(y, z, core)))
        for y in range(4)
        for z in range(2)
        for core in range(2)
    ]


Y_UP = chip_moves(lambda y, z, core: (y + 1, z, core))
Y_DOWN = chip_moves(lambda y, z, core: (y - 1, z, core))
Z_SWAP = chip_moves(lambda y, z, core: (y, z + 1, core))
CORE_SWAP = chip_moves(lambda y, z, core: (y, z, core + 1))
PIECE_STEPS = ((0, 0), (0, 1), (-1, 0), (1, 0), (-1, 1), (1, 1), (-2, 0), (2, 1))
LATE = 2


def sequence_moves(move):
    def index(z, x):
        return (z % 2) * 4 + x % 4

    return [(index(z, x), index(*move(z, x))) for z in range(2) for x in range(4)]


X_UP = sequence_moves(lambda z, x: (z, x + 1))
X_DOWN = sequence_moves(lambda z, x: (z, x - 1))
FAR_SWAP = sequence_moves(lambda z, x: (z + 1, x))


def after(value, *others):
    return lax.optimization_barrier((value, *others))[0]


def pass_on(value, move):
    return lax.ppermute(value, "ctx", move)


def piece_sources(my_index):
    y, z, core = my_index // 4, (my_index // 2) % 2, my_index % 2
    places = []
    for step in range(2):
        for dy, dz in PIECE_STEPS:
            places.append(((y + dy + 4) % 4) * 4 + ((z + dz) % 2) * 2 + (core + step) % 2)
    return jnp.stack(places)


def pick_kernel(count, scaled, *refs):
    onehot_ref, coef_ref = refs[0], refs[1]
    pieces, out_ref = refs[2 : 2 + count], refs[-1]
    slots = onehot_ref.shape[1]
    for p, piece in enumerate(pieces):
        picked = dot_nn(onehot_ref[p], piece[...])
        if scaled:
            picked = picked * coef_ref[p]
        out_ref[p * slots : (p + 1) * slots, :] = picked.astype(jnp.bfloat16)


def pick_rows(onehot, coef, pieces, scaled, buffer, first):
    count, (rows, width), slots = len(pieces), pieces[0].shape, onehot.shape[1]
    tile = 1024 if len(pieces) <= 2 * LATE else 512
    total = 2 * len(PIECE_STEPS) * slots
    in_specs = [
        pl.BlockSpec((count, slots, rows), lambda j: (0, 0, 0)),
        pl.BlockSpec((count, slots, 1), lambda j: (0, 0, 0)),
    ] + [pl.BlockSpec((rows, tile), lambda j: (0, j))] * count
    operands = [onehot, coef, *pieces]
    aliases = {}
    if buffer is not None:
        aliases = {len(operands): 0}
        operands.append(buffer)
        in_specs.append(pl.BlockSpec(memory_space=pl.ANY))
    block = count * slots
    return pl.pallas_call(
        lambda *refs: pick_kernel(count, scaled, *refs),
        grid=(width // tile,),
        in_specs=in_specs,
        out_specs=pl.BlockSpec((block, tile), lambda j: (first // block, j)),
        out_shape=jax.ShapeDtypeStruct((total, width), jnp.bfloat16),
        input_output_aliases=aliases,
        cost_estimate=pl.CostEstimate(
            flops=2 * block * rows * width,
            bytes_accessed=2 * count * (rows + slots) * width,
            transcendentals=0,
        ),
        name="pick_rows",
    )(*operands)


def route_slots(coef_rows, capacity):
    present = coef_rows > 0.0
    rank = jnp.cumsum(present.astype(jnp.int32), axis=1) - 1
    slot_ids = jnp.arange(capacity, dtype=jnp.int32)
    chosen = present[:, None, :] & (rank[:, None, :] == slot_ids[None, :, None])
    slot_coef = jnp.sum(jnp.where(chosen, coef_rows[:, None, :], 0.0), axis=2, keepdims=True)
    return chosen.astype(jnp.bfloat16), slot_coef


def term_kernel(per_step, homes, order_ref, delta_ref, *refs):
    rows, out_refs = refs[:per_step], refs[per_step:]
    step = pl.program_id(0)
    values = [dot_nn(delta_ref[...], row[...]).astype(jnp.bfloat16) for row in rows]
    for t in range(len(homes) // per_step):

        @pl.when(step == t)
        def _(t=t):
            for u, value in enumerate(values):
                array, place = homes[t * per_step + u]
                out_refs[array][place] = value


def weight_terms(order, delta, rows, stacks):
    count, per_step = order.shape[0], 4
    hidden, slots = delta.shape
    tile = rows.shape[1] // count
    homes = [(a, p) for a, depth in enumerate(stacks) for p in range(depth)]
    return pl.pallas_call(
        lambda *refs: term_kernel(per_step, homes, *refs),
        grid_spec=pltpu.PrefetchScalarGridSpec(
            num_scalar_prefetch=1,
            grid=(count // per_step,),
            in_specs=[pl.BlockSpec((hidden, slots), lambda j, order_ref: (0, 0))]
            + [
                pl.BlockSpec(
                    (slots, tile), lambda j, order_ref, u=u: (0, order_ref[j * per_step + u])
                )
                for u in range(per_step)
            ],
            out_specs=[
                pl.BlockSpec((depth, hidden, tile), lambda j, order_ref: (0, 0, 0))
                for depth in stacks
            ],
        ),
        out_shape=[jax.ShapeDtypeStruct((depth, hidden, tile), jnp.bfloat16) for depth in stacks],
        cost_estimate=pl.CostEstimate(flops=0, bytes_accessed=1_000_000, transcendentals=0),
        name="weight_terms",
    )(order, delta, *([rows] * per_step))


def term_order(steps):
    place = lax.axis_index("dp")
    z, x = place // 4, place % 4
    return jnp.stack([((z + dz) % 2) * 4 + (x + dx) % 4 for dx, dz in steps]).astype(jnp.int32)


RING_FIRST = ((2, 0), (1, 1), (2, 1), (3, 0), (1, 0), (3, 1), (0, 1), (0, 0))
ACROSS_FIRST = ((2, 1), (1, 1), (3, 1), (0, 1), (2, 0), (1, 0), (3, 0), (0, 0))


def add_terms(*terms):
    total = terms[0].astype(jnp.float32)
    for term in terms[1:]:
        total = total + term.astype(jnp.float32)
    return total


def sum_ring_first(upward, downward, rest):
    from_below = lax.ppermute(upward, "dp", X_UP)
    from_above = lax.ppermute(downward, "dp", X_DOWN)
    send_up = add_terms(rest[0], from_below[0]).astype(jnp.bfloat16)
    send_down = add_terms(rest[1], from_above[0]).astype(jnp.bfloat16)
    up_same = lax.ppermute(send_up, "dp", X_UP)
    down_other = lax.ppermute(send_down, "dp", X_DOWN)
    across = add_terms(rest[2], from_below[1], down_other).astype(jnp.bfloat16)
    arrived = lax.ppermute(across, "dp", FAR_SWAP)
    return add_terms(rest[3], up_same, from_above[1], arrived).T[None]


def sum_across_first(other, same):
    arrived = lax.ppermute(other, "dp", FAR_SWAP)
    cut = same.shape[1] // 2

    def kept(place, rows):
        return add_terms(same[place, rows], arrived[place, rows])

    head, tail = slice(0, cut), slice(cut, None)
    up_far = lax.ppermute(kept(0, head).astype(jnp.bfloat16), "dp", X_UP)
    down_far = lax.ppermute(kept(0, tail).astype(jnp.bfloat16), "dp", X_DOWN)
    next_sum = jnp.concatenate([kept(1, head) + up_far.astype(jnp.float32), kept(1, tail)])
    back_sum = jnp.concatenate([kept(2, head), kept(2, tail) + down_far.astype(jnp.float32)])
    from_below = lax.ppermute(next_sum.astype(jnp.bfloat16), "dp", X_UP)
    from_above = lax.ppermute(back_sum.astype(jnp.bfloat16), "dp", X_DOWN)
    return add_terms(kept(3, slice(None)), from_below, from_above).T[None]


def per_device(
    query_rows,
    key_rows,
    value_rows,
    block_lists,
    block_lengths,
    out_weight,
    expert_input,
    layer_grad,
    route_experts,
    route_weight,
    gate_weight,
    up_weight,
    down_weight,
):
    ctx_count = lax.axis_size("ctx")
    my_index = lax.axis_index("ctx")
    tokens_here = expert_input[0]
    grads_here = layer_grad[0]
    capacity = min(BLK, BLK * TOPK * 4 // (3 * ctx_count))

    all_experts = jnp.arange(ctx_count, dtype=jnp.int32)
    matches = route_experts[0][None, :, :] == all_experts[:, None, None]
    coef_out = jnp.sum(jnp.where(matches, route_weight[0][None], 0.0), axis=2)
    coef_in = lax.all_to_all(coef_out, "ctx", split_axis=0, concat_axis=0, tiled=True)
    onehot, slot_coef = route_slots(coef_in[piece_sources(my_index)], capacity)
    keep = len(PIECE_STEPS) - LATE
    halves = (slice(0, keep), slice(keep + LATE, 2 * keep + LATE))
    tails = (slice(keep, keep + LATE), slice(2 * keep + LATE, None))
    onehot, slot_coef = (
        jnp.concatenate([v[part] for part in halves + tails]) for v in (onehot, slot_coef)
    )

    early = 2 * keep

    def early_pick(mine, others, scaled, *gates):
        slots = after(onehot[:early], *gates)
        return pick_rows(slots, slot_coef[:early], mine + others, scaled, None, 0)

    def late_pick(mine, others, scaled, buffer, *gates):
        slots = after(onehot[early:], *gates)
        first = early * capacity
        return pick_rows(slots, slot_coef[early:], mine + others, scaled, buffer, first)

    beside, below, above = (pass_on(tokens_here, move) for move in (Z_SWAP, Y_UP, Y_DOWN))
    below_beside, above_beside = pass_on(beside, Y_UP), pass_on(beside, Y_DOWN)
    far, far_beside = pass_on(below, Y_UP), pass_on(above_beside, Y_DOWN)
    near_rows = [tokens_here, beside, below, above, below_beside, above_beside]
    near_others = [pass_on(piece, CORE_SWAP) for piece in near_rows]
    far_rows = [far, far_beside]
    far_others = [pass_on(piece, CORE_SWAP) for piece in far_rows]

    packed = pack_rows(
        query_rows[0], key_rows[0], value_rows[0], after(grads_here, beside, below), out_weight
    )

    grads_out = after(grads_here, below_beside, above_beside)
    g_beside, g_below, g_above = (pass_on(grads_out, move) for move in (Z_SWAP, Y_UP, Y_DOWN))
    buffer = early_pick(near_rows, near_others, False, packed)
    beside_out, below_out = after(g_beside, buffer), after(g_below, buffer)
    g_below_beside, g_above_beside = pass_on(beside_out, Y_UP), pass_on(beside_out, Y_DOWN)
    g_far = pass_on(below_out, Y_UP)
    rows_in = late_pick(far_rows, far_others, False, buffer)
    gate_pre = dot_nn(rows_in, gate_weight[0])
    g_far_beside = pass_on(after(g_above_beside, gate_pre), Y_DOWN)
    up_pre = dot_nn(rows_in, up_weight[0])
    gate_sig = jax.nn.sigmoid(gate_pre)
    gate_act = gate_pre * gate_sig
    hidden = (gate_act * up_pre).astype(jnp.bfloat16)
    g_near = [grads_here, g_beside, g_below, g_above, g_below_beside, g_above_beside]
    g_near_others = [pass_on(piece, CORE_SWAP) for piece in g_near]
    g_buffer = early_pick(g_near, g_near_others, True)
    g_fars = [g_far, g_far_beside]
    g_far_others = [pass_on(piece, CORE_SWAP) for piece in g_fars]
    grads_in = late_pick(g_fars, g_far_others, True, g_buffer)

    ring_order, across_order = term_order(RING_FIRST), term_order(ACROSS_FIRST)
    down_terms = weight_terms(ring_order, hidden.T, grads_in, (2, 2, 4))
    down_grad = sum_ring_first(*down_terms)
    hidden_grad = dot_nn(after(grads_in, down_terms[0]), down_weight[0])
    gate_delta = (hidden_grad * up_pre * gate_sig * (1.0 + gate_pre * (1.0 - gate_sig))).astype(
        jnp.bfloat16
    )
    up_delta = (hidden_grad * gate_act).astype(jnp.bfloat16)
    packed = after(packed, gate_delta)
    head_rows = lax.all_to_all(packed, "ctx", split_axis=0, concat_axis=0, tiled=True)
    up_terms = weight_terms(across_order, up_delta.T, rows_in, (4, 4))
    up_grad = sum_across_first(*up_terms)
    gate_terms = weight_terms(ring_order, after(gate_delta, up_terms[0]).T, rows_in, (2, 2, 4))
    gate_grad = sum_ring_first(*gate_terms)

    half = (my_index % 2).astype(jnp.int32).reshape(1)
    head_rows = after(head_rows, gate_terms[0])
    grad_rows = attention_rows(
        block_lists.reshape(-1), block_lengths.reshape(-1), half, head_rows
    )
    returned = lax.all_to_all(grad_rows, "ctx", split_axis=0, concat_axis=0, tiled=True)
    query_grad, key_grad, value_grad = unpack_rows(returned)
    return (query_grad[None], key_grad[None], value_grad[None], gate_grad, up_grad, down_grad)


def solution(mesh):
    in_specs = (
        P("dp", "ctx", None),
        P("dp", "ctx", None),
        P("dp", "ctx", None),
        P("dp", None, None),
        P("dp", None),
        P(),
        P("dp", "ctx", None),
        P("dp", "ctx", None),
        P("dp", "ctx", None),
        P("dp", "ctx", None),
        P("ctx", None, None),
        P("ctx", None, None),
        P("ctx", None, None),
    )
    out_specs = (
        P("dp", "ctx", None),
        P("dp", "ctx", None),
        P("dp", "ctx", None),
        P("ctx", "dp", None),
        P("ctx", "dp", None),
        P("ctx", "dp", None),
    )
    return jax.shard_map(
        per_device, mesh=mesh, in_specs=in_specs, out_specs=out_specs, check_vma=False
    )
```

```python
import math

import jax
import jax.numpy as jnp
from jax import lax
from jax.experimental import pallas as pl
from jax.experimental.pallas import tpu as pltpu
from jax.sharding import PartitionSpec as P


HEADS = 8
HD = 128
TOPK = 6
BLK = 128
NSEL = 4
HALF = BLK // 2
TOGETHER = 2


def dot_nt(a, b):
    return lax.dot_general(a, b, (((1,), (1,)), ((), ())), preferred_element_type=jnp.float32)


def dot_nn(a, b):
    return lax.dot_general(a, b, (((1,), (0,)), ((), ())), preferred_element_type=jnp.float32)


def dot_tn(a, b):
    return lax.dot_general(a, b, (((0,), (0,)), ((), ())), preferred_element_type=jnp.float32)


def pack_kernel(q_ref, k_ref, v_ref, g_ref, w_ref, out_ref):
    out_grad = dot_nt(g_ref[...], w_ref[...]).astype(jnp.bfloat16)
    for head in range(2):
        cols = slice(head * HD, (head + 1) * HD)
        for half in range(2):
            rows, place = slice(half * HALF, (half + 1) * HALF), 2 * head + half
            out_ref[place, 0:BLK, :] = k_ref[:, cols]
            out_ref[place, BLK : 2 * BLK, :] = v_ref[:, cols]
            out_ref[place, 2 * BLK : 2 * BLK + HALF, :] = q_ref[rows, cols]
            out_ref[place, 2 * BLK + HALF :, :] = out_grad[rows, cols]


def pack_rows(queries, keys, values, grads, out_weight):
    width = out_weight.shape[1]
    col = pl.BlockSpec((BLK, 2 * HD), lambda h: (0, h))
    return pl.pallas_call(
        pack_kernel,
        grid=(HEADS // 2,),
        in_specs=[
            col,
            col,
            col,
            pl.BlockSpec((BLK, width), lambda h: (0, 0)),
            pl.BlockSpec((2 * HD, width), lambda h: (h, 0)),
        ],
        out_specs=pl.BlockSpec((4, 3 * BLK, HD), lambda h: (h, 0, 0)),
        out_shape=jax.ShapeDtypeStruct((2 * HEADS, 3 * BLK, HD), jnp.bfloat16),
        cost_estimate=pl.CostEstimate(
            flops=2 * BLK * HEADS * HD * width, bytes_accessed=7_000_000, transcendentals=0
        ),
        name="pack_rows",
    )(queries, keys, values, grads, out_weight)


def attention_kernel(lists_ref, lengths_ref, half_ref, rows_ref, out_ref, key_acc, value_acc):
    inv_root = 1.0 / math.sqrt(HD)
    blocks = rows_ref.shape[0]
    key_acc[...] = jnp.zeros_like(key_acc)
    value_acc[...] = jnp.zeros_like(value_acc)
    query_at = lax.broadcasted_iota(jnp.int32, (HALF, BLK), 0) + half_ref[0] * HALF
    key_at = lax.broadcasted_iota(jnp.int32, (HALF, BLK), 1)

    def score(i):
        query = rows_ref[i, 2 * BLK : 2 * BLK + HALF, :]
        listed = [lists_ref[i * NSEL + n] for n in range(NSEL)]
        scores = []
        for n, block in enumerate(listed):
            limit = lengths_ref[block]
            for earlier in listed[:n]:
                limit = jnp.where(earlier == block, 0, limit)
            reach = jnp.where(block < i, BLK, 0)
            allowed = (key_at < limit) & (key_at <= query_at + reach)
            raw = dot_nt(query, rows_ref[block, 0:BLK, :]) * inv_root
            scores.append(jnp.where(allowed, raw, -jnp.inf))
        return listed, scores

    def normalize(scores):
        top = scores[0]
        for part in scores[1:]:
            top = jnp.maximum(top, part)
        row_max = jnp.max(top, axis=1, keepdims=True)
        total = jnp.exp(scores[0] - row_max)
        for part in scores[1:]:
            total = total + jnp.exp(part - row_max)
        log_total = row_max + jnp.log(jnp.sum(total, axis=1, keepdims=True))
        return [jnp.exp(part - log_total) for part in scores]

    def terms(i, listed, probs):
        query = rows_ref[i, 2 * BLK : 2 * BLK + HALF, :]
        grad = rows_ref[i, 2 * BLK + HALF :, :]
        lows = [prob.astype(jnp.bfloat16) for prob in probs]
        head = dot_nn(lows[0], rows_ref[listed[0], BLK : 2 * BLK, :])
        for n in range(1, NSEL):
            head = head + dot_nn(lows[n], rows_ref[listed[n], BLK : 2 * BLK, :])
        prob_grads = [dot_nt(grad, rows_ref[block, BLK : 2 * BLK, :]) for block in listed]
        row_delta = jnp.sum(head * grad.astype(jnp.float32), axis=1, keepdims=True)
        dscores = [
            (prob * (prob_grad - row_delta)).astype(jnp.bfloat16)
            for prob, prob_grad in zip(probs, prob_grads)
        ]
        query_sum = dot_nn(dscores[0], rows_ref[listed[0], 0:BLK, :])
        for n in range(1, NSEL):
            query_sum = query_sum + dot_nn(dscores[n], rows_ref[listed[n], 0:BLK, :])
        key_terms = [dot_tn(dscore, query) for dscore in dscores]
        value_terms = [dot_tn(low, grad) for low in lows]
        return query_sum, key_terms, value_terms

    def some_blocks(group, carry):
        rows = [group * TOGETHER + u for u in range(TOGETHER)]
        scored = [score(i) for i in rows]
        probs = [normalize(scores) for _, scores in scored]
        results = [terms(i, scored[u][0], probs[u]) for u, i in enumerate(rows)]
        for u, i in enumerate(rows):
            query_sum, key_terms, value_terms = results[u]
            out_ref[i, 2 * BLK :, :] = (query_sum * inv_root).astype(jnp.bfloat16)
            for n, block in enumerate(scored[u][0]):
                key_acc[block] += key_terms[n]
                value_acc[block] += value_terms[n]
        return carry

    lax.fori_loop(0, blocks // TOGETHER, some_blocks, 0)
    for i in range(blocks):
        out_ref[i, 0:BLK, :] = (key_acc[i] * inv_root).astype(jnp.bfloat16)
        out_ref[i, BLK : 2 * BLK, :] = value_acc[i].astype(jnp.bfloat16)


def attention_rows(lists, lengths, half, rows):
    blocks = rows.shape[0]
    smem = pl.BlockSpec(memory_space=pltpu.SMEM)
    vmem = pl.BlockSpec(memory_space=pltpu.VMEM)
    return pl.pallas_call(
        attention_kernel,
        in_specs=[smem, smem, smem, vmem],
        out_specs=vmem,
        out_shape=jax.ShapeDtypeStruct((blocks, 2 * BLK + HALF, HD), jnp.bfloat16),
        scratch_shapes=[
            pltpu.VMEM((blocks, BLK, HD), jnp.float32),
            pltpu.VMEM((blocks, BLK, HD), jnp.float32),
        ],
        cost_estimate=pl.CostEstimate(flops=0, bytes_accessed=3_000_000, transcendentals=0),
        name="attention_rows",
    )(lists, lengths, half, rows)


def unpack_kernel(rows_ref, query_ref, key_ref, value_ref):
    for h in range(HEADS):
        cols = slice(h * HD, (h + 1) * HD)

        def both(rows):
            first = rows_ref[2 * h, rows, :].astype(jnp.float32)
            return (first + rows_ref[2 * h + 1, rows, :].astype(jnp.float32)).astype(jnp.bfloat16)

        key_ref[:, cols] = both(slice(0, BLK))
        value_ref[:, cols] = both(slice(BLK, 2 * BLK))
        query_ref[0:HALF, cols] = rows_ref[2 * h, 2 * BLK :, :]
        query_ref[HALF:BLK, cols] = rows_ref[2 * h + 1, 2 * BLK :, :]


def unpack_rows(rows):
    vmem = pl.BlockSpec(memory_space=pltpu.VMEM)
    shape = jax.ShapeDtypeStruct((BLK, HEADS * HD), jnp.bfloat16)
    return pl.pallas_call(
        unpack_kernel,
        in_specs=[vmem],
        out_specs=(vmem, vmem, vmem),
        out_shape=(shape, shape, shape),
        cost_estimate=pl.CostEstimate(flops=0, bytes_accessed=2_000_000, transcendentals=0),
        name="unpack_rows",
    )(rows)


def chip_moves(move):
    def index(y, z, core):
        return (y % 4) * 4 + (z % 2) * 2 + core % 2

    return [
        (index(y, z, core), index(*move(y, z, core)))
        for y in range(4)
        for z in range(2)
        for core in range(2)
    ]


Y_UP = chip_moves(lambda y, z, core: (y + 1, z, core))
Y_DOWN = chip_moves(lambda y, z, core: (y - 1, z, core))
Z_SWAP = chip_moves(lambda y, z, core: (y, z + 1, core))
CORE_SWAP = chip_moves(lambda y, z, core: (y, z, core + 1))
PIECE_STEPS = ((0, 0), (0, 1), (-1, 0), (1, 0), (-1, 1), (1, 1), (-2, 0), (2, 1))
LATE = 2


def sequence_moves(move):
    def index(z, x):
        return (z % 2) * 4 + x % 4

    return [(index(z, x), index(*move(z, x))) for z in range(2) for x in range(4)]


X_UP = sequence_moves(lambda z, x: (z, x + 1))
X_DOWN = sequence_moves(lambda z, x: (z, x - 1))
FAR_SWAP = sequence_moves(lambda z, x: (z + 1, x))


def pass_on(value, move):
    return lax.ppermute(value, "ctx", move)


def piece_sources(my_index):
    y, z, core = my_index // 4, (my_index // 2) % 2, my_index % 2
    places = []
    for step in range(2):
        for dy, dz in PIECE_STEPS:
            places.append(((y + dy + 4) % 4) * 4 + ((z + dz) % 2) * 2 + (core + step) % 2)
    return jnp.stack(places)


def pick_kernel(count, scaled, *refs):
    onehot_ref, coef_ref = refs[0], refs[1]
    pieces, out_ref = refs[2 : 2 + count], refs[-1]
    slots = onehot_ref.shape[1]
    for p, piece in enumerate(pieces):
        picked = dot_nn(onehot_ref[p], piece[...])
        if scaled:
            picked = picked * coef_ref[p]
        out_ref[p * slots : (p + 1) * slots, :] = picked.astype(jnp.bfloat16)


def pick_rows(onehot, coef, pieces, scaled, buffer, first):
    count, (rows, width), slots = len(pieces), pieces[0].shape, onehot.shape[1]
    tile = 1024 if len(pieces) <= 2 * LATE else 512
    total = 2 * len(PIECE_STEPS) * slots
    in_specs = [
        pl.BlockSpec((count, slots, rows), lambda j: (0, 0, 0)),
        pl.BlockSpec((count, slots, 1), lambda j: (0, 0, 0)),
    ] + [pl.BlockSpec((rows, tile), lambda j: (0, j))] * count
    operands = [onehot, coef, *pieces]
    aliases = {}
    if buffer is not None:
        aliases = {len(operands): 0}
        operands.append(buffer)
        in_specs.append(pl.BlockSpec(memory_space=pl.ANY))
    block = count * slots
    return pl.pallas_call(
        lambda *refs: pick_kernel(count, scaled, *refs),
        grid=(width // tile,),
        in_specs=in_specs,
        out_specs=pl.BlockSpec((block, tile), lambda j: (first // block, j)),
        out_shape=jax.ShapeDtypeStruct((total, width), jnp.bfloat16),
        input_output_aliases=aliases,
        cost_estimate=pl.CostEstimate(
            flops=2 * block * rows * width,
            bytes_accessed=2 * count * (rows + slots) * width,
            transcendentals=0,
        ),
        name="pick_rows",
    )(*operands)


def route_slots(coef_rows, capacity):
    present = coef_rows > 0.0
    rank = jnp.cumsum(present.astype(jnp.int32), axis=1) - 1
    slot_ids = jnp.arange(capacity, dtype=jnp.int32)
    chosen = present[:, None, :] & (rank[:, None, :] == slot_ids[None, :, None])
    slot_coef = jnp.sum(jnp.where(chosen, coef_rows[:, None, :], 0.0), axis=2, keepdims=True)
    return chosen.astype(jnp.bfloat16), slot_coef


def term_kernel(per_step, homes, order_ref, delta_ref, *refs):
    rows, out_refs = refs[:per_step], refs[per_step:]
    step = pl.program_id(0)
    values = [dot_nn(delta_ref[...], row[...]).astype(jnp.bfloat16) for row in rows]
    for t in range(len(homes) // per_step):

        @pl.when(step == t)
        def _(t=t):
            for u, value in enumerate(values):
                array, place = homes[t * per_step + u]
                out_refs[array][place] = value


def weight_terms(order, delta, rows, stacks):
    count, per_step = order.shape[0], 4
    hidden, slots = delta.shape
    tile = rows.shape[1] // count
    homes = [(a, p) for a, depth in enumerate(stacks) for p in range(depth)]
    return pl.pallas_call(
        lambda *refs: term_kernel(per_step, homes, *refs),
        grid_spec=pltpu.PrefetchScalarGridSpec(
            num_scalar_prefetch=1,
            grid=(count // per_step,),
            in_specs=[pl.BlockSpec((hidden, slots), lambda j, order_ref: (0, 0))]
            + [
                pl.BlockSpec(
                    (slots, tile), lambda j, order_ref, u=u: (0, order_ref[j * per_step + u])
                )
                for u in range(per_step)
            ],
            out_specs=[
                pl.BlockSpec((depth, hidden, tile), lambda j, order_ref: (0, 0, 0))
                for depth in stacks
            ],
        ),
        out_shape=[jax.ShapeDtypeStruct((depth, hidden, tile), jnp.bfloat16) for depth in stacks],
        cost_estimate=pl.CostEstimate(flops=0, bytes_accessed=1_000_000, transcendentals=0),
        name="weight_terms",
    )(order, delta, *([rows] * per_step))


def term_order(steps):
    place = lax.axis_index("dp")
    z, x = place // 4, place % 4
    return jnp.stack([((z + dz) % 2) * 4 + (x + dx) % 4 for dx, dz in steps]).astype(jnp.int32)


RING_FIRST = ((2, 0), (1, 1), (2, 1), (3, 0), (1, 0), (3, 1), (0, 1), (0, 0))
ACROSS_FIRST = ((2, 1), (1, 1), (3, 1), (0, 1), (2, 0), (1, 0), (3, 0), (0, 0))


def add_terms(*terms):
    total = terms[0].astype(jnp.float32)
    for term in terms[1:]:
        total = total + term.astype(jnp.float32)
    return total


def sum_ring_first(upward, downward, rest):
    from_below = lax.ppermute(upward, "dp", X_UP)
    from_above = lax.ppermute(downward, "dp", X_DOWN)
    send_up = add_terms(rest[0], from_below[0]).astype(jnp.bfloat16)
    send_down = add_terms(rest[1], from_above[0]).astype(jnp.bfloat16)
    up_same = lax.ppermute(send_up, "dp", X_UP)
    down_other = lax.ppermute(send_down, "dp", X_DOWN)
    across = add_terms(rest[2], from_below[1], down_other).astype(jnp.bfloat16)
    arrived = lax.ppermute(across, "dp", FAR_SWAP)
    return add_terms(rest[3], up_same, from_above[1], arrived).T[None]


def sum_across_first(other, same):
    arrived = lax.ppermute(other, "dp", FAR_SWAP)
    cut = same.shape[1] // 2

    def kept(place, rows):
        return add_terms(same[place, rows], arrived[place, rows])

    head, tail = slice(0, cut), slice(cut, None)
    far_head = kept(0, head).astype(jnp.bfloat16)
    far_tail = kept(0, tail).astype(jnp.bfloat16)
    up_far = lax.ppermute(far_head, "dp", X_UP)
    down_far = lax.ppermute(far_tail, "dp", X_DOWN)
    next_sum = jnp.concatenate([kept(1, head) + up_far.astype(jnp.float32), kept(1, tail)])
    back_sum = jnp.concatenate([kept(2, head), kept(2, tail) + down_far.astype(jnp.float32)])
    from_below = lax.ppermute(next_sum.astype(jnp.bfloat16), "dp", X_UP)
    from_above = lax.ppermute(back_sum.astype(jnp.bfloat16), "dp", X_DOWN)
    return add_terms(kept(3, slice(None)), from_below, from_above).T[None]


def per_device(
    query_rows,
    key_rows,
    value_rows,
    block_lists,
    block_lengths,
    out_weight,
    expert_input,
    layer_grad,
    route_experts,
    route_weight,
    gate_weight,
    up_weight,
    down_weight,
):
    ctx_count = lax.axis_size("ctx")
    my_index = lax.axis_index("ctx")
    tokens_here = expert_input[0]
    grads_here = layer_grad[0]
    capacity = min(BLK, BLK * TOPK * 4 // (3 * ctx_count))

    all_experts = jnp.arange(ctx_count, dtype=jnp.int32)
    matches = route_experts[0][None, :, :] == all_experts[:, None, None]
    coef_out = jnp.sum(jnp.where(matches, route_weight[0][None], 0.0), axis=2)
    coef_in = lax.all_to_all(coef_out, "ctx", split_axis=0, concat_axis=0, tiled=True)
    keep = len(PIECE_STEPS) - LATE
    early = 2 * keep
    halves = (slice(0, keep), slice(keep + LATE, 2 * keep + LATE))
    tails = (slice(keep, keep + LATE), slice(2 * keep + LATE, None))
    onehot, slot_coef = route_slots(coef_in[piece_sources(my_index)], capacity)
    onehot, slot_coef = (
        jnp.concatenate([v[part] for part in halves + tails]) for v in (onehot, slot_coef)
    )

    def early_pick(mine, others, scaled):
        return pick_rows(onehot[:early], slot_coef[:early], mine + others, scaled, None, 0)

    def late_pick(mine, others, scaled, buffer):
        first = early * capacity
        return pick_rows(onehot[early:], slot_coef[early:], mine + others, scaled, buffer, first)

    beside, below, above = (pass_on(tokens_here, move) for move in (Z_SWAP, Y_UP, Y_DOWN))
    below_beside = pass_on(beside, Y_UP)
    above_beside = pass_on(beside, Y_DOWN)
    far, far_beside = pass_on(below, Y_UP), pass_on(above_beside, Y_DOWN)
    near_rows = [tokens_here, beside, below, above, below_beside, above_beside]
    near_others = [pass_on(piece, CORE_SWAP) for piece in near_rows]
    far_rows = [far, far_beside]
    far_others = [pass_on(piece, CORE_SWAP) for piece in far_rows]

    packed = pack_rows(query_rows[0], key_rows[0], value_rows[0], grads_here, out_weight)

    g_beside, g_below, g_above = (pass_on(grads_here, move) for move in (Z_SWAP, Y_UP, Y_DOWN))
    g_below_beside, g_above_beside = pass_on(g_beside, Y_UP), pass_on(g_beside, Y_DOWN)
    g_far = pass_on(g_below, Y_UP)
    g_far_beside = pass_on(g_above_beside, Y_DOWN)
    buffer = early_pick(near_rows, near_others, False)
    rows_in = late_pick(far_rows, far_others, False, buffer)
    gate_pre = lax.optimization_barrier(dot_nn(rows_in, gate_weight[0]))
    gate_sig = jax.nn.sigmoid(gate_pre)
    gate_act = gate_pre * gate_sig
    up_pre = dot_nn(rows_in, up_weight[0])
    hidden = (gate_act * up_pre).astype(jnp.bfloat16)
    up_pre, hidden = lax.optimization_barrier((up_pre, hidden))
    g_near = [grads_here, g_beside, g_below, g_above, g_below_beside, g_above_beside]
    g_near_others = [pass_on(piece, CORE_SWAP) for piece in g_near]
    g_buffer = early_pick(g_near, g_near_others, True)
    g_fars = [g_far, g_far_beside]
    g_far_others = [pass_on(piece, CORE_SWAP) for piece in g_fars]
    grads_in = late_pick(g_fars, g_far_others, True, g_buffer)

    ring_order, across_order = term_order(RING_FIRST), term_order(ACROSS_FIRST)
    down_terms = weight_terms(ring_order, hidden.T, grads_in, (2, 2, 4))
    down_grad = sum_ring_first(*down_terms)
    head_rows = lax.all_to_all(packed, "ctx", split_axis=0, concat_axis=0, tiled=True)
    later_grads = lax.optimization_barrier((grads_in, down_terms[0]))[0]
    hidden_grad = dot_nn(later_grads, down_weight[0])
    gate_delta = (
        hidden_grad * up_pre * gate_sig * (1.0 + gate_pre * (1.0 - gate_sig))
    ).astype(jnp.bfloat16)
    up_delta = (hidden_grad * gate_act).astype(jnp.bfloat16)
    up_grad = sum_across_first(*weight_terms(across_order, up_delta.T, rows_in, (4, 4)))
    gate_terms = weight_terms(ring_order, gate_delta.T, rows_in, (2, 2, 4))
    gate_grad = sum_ring_first(*gate_terms)

    half = (my_index % 2).astype(jnp.int32).reshape(1)
    grad_rows = attention_rows(block_lists.reshape(-1), block_lengths.reshape(-1), half, head_rows)
    returned = lax.all_to_all(grad_rows, "ctx", split_axis=0, concat_axis=0, tiled=True)
    query_grad, key_grad, value_grad = unpack_rows(returned)
    return (query_grad[None], key_grad[None], value_grad[None], gate_grad, up_grad, down_grad)


def solution(mesh):
    in_specs = (
        P("dp", "ctx", None),
        P("dp", "ctx", None),
        P("dp", "ctx", None),
        P("dp", None, None),
        P("dp", None),
        P(),
        P("dp", "ctx", None),
        P("dp", "ctx", None),
        P("dp", "ctx", None),
        P("dp", "ctx", None),
        P("ctx", None, None),
        P("ctx", None, None),
        P("ctx", None, None),
    )
    out_specs = (
        P("dp", "ctx", None),
        P("dp", "ctx", None),
        P("dp", "ctx", None),
        P("ctx", "dp", None),
        P("ctx", "dp", None),
        P("ctx", "dp", None),
    )
    return jax.shard_map(
        per_device, mesh=mesh, in_specs=in_specs, out_specs=out_specs, check_vma=False
    )
```

```python
import math

import jax
import jax.numpy as jnp
from jax import lax
from jax.experimental import pallas as pl
from jax.experimental.pallas import tpu as pltpu
from jax.sharding import PartitionSpec as P


HEADS = 8
HD = 128
TOPK = 6
BLK = 128
NSEL = 4
HALF = BLK // 2
TOGETHER = 4


def dot_nt(a, b):
    return lax.dot_general(a, b, (((1,), (1,)), ((), ())), preferred_element_type=jnp.float32)


def dot_nn(a, b):
    return lax.dot_general(a, b, (((1,), (0,)), ((), ())), preferred_element_type=jnp.float32)


def dot_tn(a, b):
    return lax.dot_general(a, b, (((0,), (0,)), ((), ())), preferred_element_type=jnp.float32)


def pack_kernel(q_ref, k_ref, v_ref, g_ref, w_ref, out_ref):
    out_grad = dot_nt(g_ref[...], w_ref[...]).astype(jnp.bfloat16)
    for head in range(2):
        cols = slice(head * HD, (head + 1) * HD)
        for half in range(2):
            rows, place = slice(half * HALF, (half + 1) * HALF), 2 * head + half
            out_ref[place, 0:BLK, :] = k_ref[:, cols]
            out_ref[place, BLK : 2 * BLK, :] = v_ref[:, cols]
            out_ref[place, 2 * BLK : 2 * BLK + HALF, :] = q_ref[rows, cols]
            out_ref[place, 2 * BLK + HALF :, :] = out_grad[rows, cols]


def pack_rows(queries, keys, values, grads, out_weight):
    width = out_weight.shape[1]
    col = pl.BlockSpec((BLK, 2 * HD), lambda h: (0, h))
    return pl.pallas_call(
        pack_kernel,
        grid=(HEADS // 2,),
        in_specs=[
            col,
            col,
            col,
            pl.BlockSpec((BLK, width), lambda h: (0, 0)),
            pl.BlockSpec((2 * HD, width), lambda h: (h, 0)),
        ],
        out_specs=pl.BlockSpec((4, 3 * BLK, HD), lambda h: (h, 0, 0)),
        out_shape=jax.ShapeDtypeStruct((2 * HEADS, 3 * BLK, HD), jnp.bfloat16),
        cost_estimate=pl.CostEstimate(
            flops=2 * BLK * HEADS * HD * width, bytes_accessed=7_000_000, transcendentals=0
        ),
        name="pack_rows",
    )(queries, keys, values, grads, out_weight)


def attention_kernel(lists_ref, lengths_ref, half_ref, rows_ref, out_ref, key_acc, value_acc):
    inv_root = 1.0 / math.sqrt(HD)
    blocks = rows_ref.shape[0]
    key_acc[...] = jnp.zeros_like(key_acc)
    value_acc[...] = jnp.zeros_like(value_acc)
    query_at = lax.broadcasted_iota(jnp.int32, (HALF, BLK), 0) + half_ref[0] * HALF
    key_at = lax.broadcasted_iota(jnp.int32, (HALF, BLK), 1)

    def score(i):
        query = rows_ref[i, 2 * BLK : 2 * BLK + HALF, :]
        listed = [lists_ref[i * NSEL + n] for n in range(NSEL)]
        scores = []
        for n, block in enumerate(listed):
            limit = lengths_ref[block]
            for earlier in listed[:n]:
                limit = jnp.where(earlier == block, 0, limit)
            reach = jnp.where(block < i, BLK, 0)
            allowed = (key_at < limit) & (key_at <= query_at + reach)
            raw = dot_nt(query, rows_ref[block, 0:BLK, :]) * inv_root
            scores.append(jnp.where(allowed, raw, -jnp.inf))
        return listed, scores

    def normalize(scores):
        top = scores[0]
        for part in scores[1:]:
            top = jnp.maximum(top, part)
        row_max = jnp.max(top, axis=1, keepdims=True)
        total = jnp.exp(scores[0] - row_max)
        for part in scores[1:]:
            total = total + jnp.exp(part - row_max)
        log_total = row_max + jnp.log(jnp.sum(total, axis=1, keepdims=True))
        return [jnp.exp(part - log_total) for part in scores]

    def terms(i, listed, probs):
        query = rows_ref[i, 2 * BLK : 2 * BLK + HALF, :]
        grad = rows_ref[i, 2 * BLK + HALF :, :]
        lows = [prob.astype(jnp.bfloat16) for prob in probs]
        head = dot_nn(lows[0], rows_ref[listed[0], BLK : 2 * BLK, :])
        for n in range(1, NSEL):
            head = head + dot_nn(lows[n], rows_ref[listed[n], BLK : 2 * BLK, :])
        prob_grads = [dot_nt(grad, rows_ref[block, BLK : 2 * BLK, :]) for block in listed]
        row_delta = jnp.sum(head * grad.astype(jnp.float32), axis=1, keepdims=True)
        dscores = [
            (prob * (prob_grad - row_delta)).astype(jnp.bfloat16)
            for prob, prob_grad in zip(probs, prob_grads)
        ]
        query_sum = dot_nn(dscores[0], rows_ref[listed[0], 0:BLK, :])
        for n in range(1, NSEL):
            query_sum = query_sum + dot_nn(dscores[n], rows_ref[listed[n], 0:BLK, :])
        key_terms = [dot_tn(dscore, query) for dscore in dscores]
        value_terms = [dot_tn(low, grad) for low in lows]
        return query_sum, key_terms, value_terms

    def some_blocks(group, carry):
        rows = [group * TOGETHER + u for u in range(TOGETHER)]
        scored = [score(i) for i in rows]
        probs = [normalize(scores) for _, scores in scored]
        results = [terms(i, scored[u][0], probs[u]) for u, i in enumerate(rows)]
        for u, i in enumerate(rows):
            query_sum, key_terms, value_terms = results[u]
            out_ref[i, 2 * BLK :, :] = (query_sum * inv_root).astype(jnp.bfloat16)
            for n, block in enumerate(scored[u][0]):
                key_acc[block] += key_terms[n]
                value_acc[block] += value_terms[n]
        return carry

    lax.fori_loop(0, blocks // TOGETHER, some_blocks, 0)
    for i in range(blocks):
        out_ref[i, 0:BLK, :] = (key_acc[i] * inv_root).astype(jnp.bfloat16)
        out_ref[i, BLK : 2 * BLK, :] = value_acc[i].astype(jnp.bfloat16)


def attention_rows(lists, lengths, half, rows):
    blocks = rows.shape[0]
    smem = pl.BlockSpec(memory_space=pltpu.SMEM)
    vmem = pl.BlockSpec(memory_space=pltpu.VMEM)
    return pl.pallas_call(
        attention_kernel,
        in_specs=[smem, smem, smem, vmem],
        out_specs=vmem,
        out_shape=jax.ShapeDtypeStruct((blocks, 2 * BLK + HALF, HD), jnp.bfloat16),
        scratch_shapes=[
            pltpu.VMEM((blocks, BLK, HD), jnp.float32),
            pltpu.VMEM((blocks, BLK, HD), jnp.float32),
        ],
        cost_estimate=pl.CostEstimate(flops=0, bytes_accessed=3_000_000, transcendentals=0),
        name="attention_rows",
    )(lists, lengths, half, rows)


def unpack_kernel(rows_ref, query_ref, key_ref, value_ref):
    for h in range(HEADS):
        cols = slice(h * HD, (h + 1) * HD)

        def both(rows):
            first = rows_ref[2 * h, rows, :].astype(jnp.float32)
            return (first + rows_ref[2 * h + 1, rows, :].astype(jnp.float32)).astype(jnp.bfloat16)

        key_ref[:, cols] = both(slice(0, BLK))
        value_ref[:, cols] = both(slice(BLK, 2 * BLK))
        query_ref[0:HALF, cols] = rows_ref[2 * h, 2 * BLK :, :]
        query_ref[HALF:BLK, cols] = rows_ref[2 * h + 1, 2 * BLK :, :]


def unpack_rows(rows):
    vmem = pl.BlockSpec(memory_space=pltpu.VMEM)
    shape = jax.ShapeDtypeStruct((BLK, HEADS * HD), jnp.bfloat16)
    return pl.pallas_call(
        unpack_kernel,
        in_specs=[vmem],
        out_specs=(vmem, vmem, vmem),
        out_shape=(shape, shape, shape),
        cost_estimate=pl.CostEstimate(flops=0, bytes_accessed=2_000_000, transcendentals=0),
        name="unpack_rows",
    )(rows)


def chip_moves(move):
    def index(y, z, core):
        return (y % 4) * 4 + (z % 2) * 2 + core % 2

    return [
        (index(y, z, core), index(*move(y, z, core)))
        for y in range(4)
        for z in range(2)
        for core in range(2)
    ]


Y_UP = chip_moves(lambda y, z, core: (y + 1, z, core))
Y_DOWN = chip_moves(lambda y, z, core: (y - 1, z, core))
Z_SWAP = chip_moves(lambda y, z, core: (y, z + 1, core))
CORE_SWAP = chip_moves(lambda y, z, core: (y, z, core + 1))
PIECE_STEPS = ((0, 0), (0, 1), (-1, 0), (1, 0), (-1, 1), (1, 1), (-2, 0), (2, 1))
LATE = 2


def sequence_moves(move):
    def index(z, x):
        return (z % 2) * 4 + x % 4

    return [(index(z, x), index(*move(z, x))) for z in range(2) for x in range(4)]


X_UP = sequence_moves(lambda z, x: (z, x + 1))
X_DOWN = sequence_moves(lambda z, x: (z, x - 1))
X_FAR = sequence_moves(lambda z, x: (z, x + 2))
X_MOVES = (X_FAR, X_UP, X_DOWN)
FAR_SWAP = sequence_moves(lambda z, x: (z + 1, x))


def pass_on(value, move):
    return lax.ppermute(value, "ctx", move)


def piece_sources(my_index):
    y, z, core = my_index // 4, (my_index // 2) % 2, my_index % 2
    places = []
    for step in range(2):
        for dy, dz in PIECE_STEPS:
            places.append(((y + dy + 4) % 4) * 4 + ((z + dz) % 2) * 2 + (core + step) % 2)
    return jnp.stack(places)


def pick_kernel(count, scaled, *refs):
    onehot_ref, coef_ref = refs[0], refs[1]
    pieces, out_ref = refs[2 : 2 + count], refs[-1]
    slots = onehot_ref.shape[1]
    for p, piece in enumerate(pieces):
        picked = dot_nn(onehot_ref[p], piece[...])
        if scaled:
            picked = picked * coef_ref[p]
        out_ref[p * slots : (p + 1) * slots, :] = picked.astype(jnp.bfloat16)


def pick_rows(onehot, coef, pieces, scaled, buffer, first):
    count, (rows, width), slots = len(pieces), pieces[0].shape, onehot.shape[1]
    tile = 1024
    total = 2 * len(PIECE_STEPS) * slots
    in_specs = [
        pl.BlockSpec((count, slots, rows), lambda j: (0, 0, 0)),
        pl.BlockSpec((count, slots, 1), lambda j: (0, 0, 0)),
    ] + [pl.BlockSpec((rows, tile), lambda j: (0, j))] * count
    operands = [onehot, coef, *pieces]
    aliases = {}
    if buffer is not None:
        aliases = {len(operands): 0}
        operands.append(buffer)
        in_specs.append(pl.BlockSpec(memory_space=pl.ANY))
    block = count * slots
    return pl.pallas_call(
        lambda *refs: pick_kernel(count, scaled, *refs),
        grid=(width // tile,),
        in_specs=in_specs,
        out_specs=pl.BlockSpec((block, tile), lambda j: (first // block, j)),
        out_shape=jax.ShapeDtypeStruct((total, width), jnp.bfloat16),
        input_output_aliases=aliases,
        cost_estimate=pl.CostEstimate(
            flops=2 * block * rows * width,
            bytes_accessed=2 * count * (rows + slots) * width,
            transcendentals=0,
        ),
        name="pick_rows",
    )(*operands)


def route_slots(coef_rows, capacity):
    present = coef_rows > 0.0
    rank = jnp.cumsum(present.astype(jnp.int32), axis=1) - 1
    slot_ids = jnp.arange(capacity, dtype=jnp.int32)
    chosen = present[:, None, :] & (rank[:, None, :] == slot_ids[None, :, None])
    slot_coef = jnp.sum(jnp.where(chosen, coef_rows[:, None, :], 0.0), axis=2, keepdims=True)
    return chosen.astype(jnp.bfloat16), slot_coef


def term_kernel(per_step, homes, order_ref, delta_ref, *refs):
    rows, out_refs = refs[:per_step], refs[per_step:]
    step = pl.program_id(0)
    values = [dot_nn(delta_ref[...], row[...]).astype(jnp.bfloat16) for row in rows]
    for t in range(len(homes) // per_step):

        @pl.when(step == t)
        def _(t=t):
            for u, value in enumerate(values):
                array, place = homes[t * per_step + u]
                out_refs[array][place] = value


def weight_terms(order, delta, rows, stacks):
    count, per_step = order.shape[0], 4
    hidden, slots = delta.shape
    tile = rows.shape[1] // count
    homes = [(a, p) for a, depth in enumerate(stacks) for p in range(depth)]
    return pl.pallas_call(
        lambda *refs: term_kernel(per_step, homes, *refs),
        grid_spec=pltpu.PrefetchScalarGridSpec(
            num_scalar_prefetch=1,
            grid=(count // per_step,),
            in_specs=[pl.BlockSpec((hidden, slots), lambda j, order_ref: (0, 0))]
            + [
                pl.BlockSpec(
                    (slots, tile), lambda j, order_ref, u=u: (0, order_ref[j * per_step + u])
                )
                for u in range(per_step)
            ],
            out_specs=[
                pl.BlockSpec((depth, hidden, tile), lambda j, order_ref: (0, 0, 0))
                for depth in stacks
            ],
        ),
        out_shape=[jax.ShapeDtypeStruct((depth, hidden, tile), jnp.bfloat16) for depth in stacks],
        cost_estimate=pl.CostEstimate(flops=0, bytes_accessed=1_000_000, transcendentals=0),
        name="weight_terms",
    )(order, delta, *([rows] * per_step))


def term_order(steps):
    place = lax.axis_index("dp")
    z, x = place // 4, place % 4
    return jnp.stack([((z + dz) % 2) * 4 + (x + dx) % 4 for dx, dz in steps]).astype(jnp.int32)


X_FIRST = ((2, 0), (2, 1), (1, 0), (1, 1), (3, 0), (3, 1), (0, 0), (0, 1))
Z_FIRST = ((2, 1), (1, 1), (3, 1), (0, 1), (2, 0), (1, 0), (3, 0), (0, 0))


def add_terms(*terms):
    total = terms[0].astype(jnp.float32)
    for term in terms[1:]:
        total = total + term.astype(jnp.float32)
    return total


def sum_x_first(*terms):
    arrived = [lax.ppermute(term, "dp", move) for term, move in zip(terms, X_MOVES)]
    parts = [terms[-1], *arrived]
    across = add_terms(*(part[1] for part in parts)).astype(jnp.bfloat16)
    other = lax.ppermute(across, "dp", FAR_SWAP)
    return add_terms(*(part[0] for part in parts), other).T[None]


def sum_z_first(other, same):
    joined = lax.ppermute(other, "dp", FAR_SWAP)
    sums = [add_terms(same[k], joined[k]).astype(jnp.bfloat16) for k in range(len(X_MOVES))]
    arrived = [lax.ppermute(term, "dp", move) for term, move in zip(sums, X_MOVES)]
    return add_terms(same[-1], joined[-1], *arrived).T[None]


def per_device(
    query_rows,
    key_rows,
    value_rows,
    block_lists,
    block_lengths,
    out_weight,
    expert_input,
    layer_grad,
    route_experts,
    route_weight,
    gate_weight,
    up_weight,
    down_weight,
):
    ctx_count = lax.axis_size("ctx")
    my_index = lax.axis_index("ctx")
    tokens_here = expert_input[0]
    grads_here = layer_grad[0]
    capacity = min(BLK, BLK * TOPK * 4 // (3 * ctx_count))

    all_experts = jnp.arange(ctx_count, dtype=jnp.int32)
    matches = route_experts[0][None, :, :] == all_experts[:, None, None]
    coef_out = jnp.sum(jnp.where(matches, route_weight[0][None], 0.0), axis=2)
    coef_in = lax.all_to_all(coef_out, "ctx", split_axis=0, concat_axis=0, tiled=True)
    keep = len(PIECE_STEPS) - LATE
    early = 2 * keep
    halves = (slice(0, keep), slice(keep + LATE, 2 * keep + LATE))
    tails = (slice(keep, keep + LATE), slice(2 * keep + LATE, None))
    onehot, slot_coef = route_slots(coef_in[piece_sources(my_index)], capacity)
    onehot, slot_coef = (
        jnp.concatenate([v[part] for part in halves + tails]) for v in (onehot, slot_coef)
    )

    def early_pick(mine, others, scaled):
        return pick_rows(onehot[:early], slot_coef[:early], mine + others, scaled, None, 0)

    def late_pick(mine, others, scaled, buffer):
        first = early * capacity
        return pick_rows(onehot[early:], slot_coef[early:], mine + others, scaled, buffer, first)

    beside, below, above = (pass_on(tokens_here, move) for move in (Z_SWAP, Y_UP, Y_DOWN))
    below_beside = pass_on(beside, Y_UP)
    above_beside = pass_on(beside, Y_DOWN)
    far, far_beside = pass_on(below, Y_UP), pass_on(above_beside, Y_DOWN)
    near_rows = [tokens_here, beside, below, above, below_beside, above_beside]
    near_others = [pass_on(piece, CORE_SWAP) for piece in near_rows]
    far_rows = [far, far_beside]
    far_others = [pass_on(piece, CORE_SWAP) for piece in far_rows]

    packed = pack_rows(query_rows[0], key_rows[0], value_rows[0], grads_here, out_weight)

    g_beside, g_below, g_above = (pass_on(grads_here, move) for move in (Z_SWAP, Y_UP, Y_DOWN))
    g_below_beside, g_above_beside = pass_on(g_beside, Y_UP), pass_on(g_beside, Y_DOWN)
    g_far = pass_on(g_below, Y_UP)
    g_far_beside = pass_on(g_above_beside, Y_DOWN)
    buffer = early_pick(near_rows, near_others, False)
    rows_in = late_pick(far_rows, far_others, False, buffer)
    gate_pre = lax.optimization_barrier(dot_nn(rows_in, gate_weight[0]))
    gate_sig = jax.nn.sigmoid(gate_pre)
    gate_act = gate_pre * gate_sig
    up_pre = dot_nn(rows_in, up_weight[0])
    hidden = (gate_act * up_pre).astype(jnp.bfloat16)
    up_pre, hidden = lax.optimization_barrier((up_pre, hidden))
    g_near = [grads_here, g_beside, g_below, g_above, g_below_beside, g_above_beside]
    g_near_others = [pass_on(piece, CORE_SWAP) for piece in g_near]
    g_buffer = early_pick(g_near, g_near_others, True)
    g_fars = [g_far, g_far_beside]
    g_far_others = [pass_on(piece, CORE_SWAP) for piece in g_fars]
    grads_in = late_pick(g_fars, g_far_others, True, g_buffer)

    x_order, z_order = term_order(X_FIRST), term_order(Z_FIRST)
    down_terms = weight_terms(x_order, hidden.T, grads_in, (2, 2, 2, 2))
    down_grad = sum_x_first(*down_terms)
    head_rows = lax.all_to_all(packed, "ctx", split_axis=0, concat_axis=0, tiled=True)
    later_grads = lax.optimization_barrier((grads_in, down_terms[0]))[0]
    hidden_grad = dot_nn(later_grads, down_weight[0])
    gate_delta = (
        hidden_grad * up_pre * gate_sig * (1.0 + gate_pre * (1.0 - gate_sig))
    ).astype(jnp.bfloat16)
    up_delta = (hidden_grad * gate_act).astype(jnp.bfloat16)
    up_grad = sum_z_first(*weight_terms(z_order, up_delta.T, rows_in, (4, 4)))
    gate_terms = weight_terms(x_order, gate_delta.T, rows_in, (2, 2, 2, 2))
    gate_grad = sum_x_first(*gate_terms)

    half = (my_index % 2).astype(jnp.int32).reshape(1)
    grad_rows = attention_rows(block_lists.reshape(-1), block_lengths.reshape(-1), half, head_rows)
    returned = lax.all_to_all(grad_rows, "ctx", split_axis=0, concat_axis=0, tiled=True)
    query_grad, key_grad, value_grad = unpack_rows(returned)
    return (query_grad[None], key_grad[None], value_grad[None], gate_grad, up_grad, down_grad)


def solution(mesh):
    in_specs = (
        P("dp", "ctx", None),
        P("dp", "ctx", None),
        P("dp", "ctx", None),
        P("dp", None, None),
        P("dp", None),
        P(),
        P("dp", "ctx", None),
        P("dp", "ctx", None),
        P("dp", "ctx", None),
        P("dp", "ctx", None),
        P("ctx", None, None),
        P("ctx", None, None),
        P("ctx", None, None),
    )
    out_specs = (
        P("dp", "ctx", None),
        P("dp", "ctx", None),
        P("dp", "ctx", None),
        P("ctx", "dp", None),
        P("ctx", "dp", None),
        P("ctx", "dp", None),
    )
    return jax.shard_map(
        per_device, mesh=mesh, in_specs=in_specs, out_specs=out_specs, check_vma=False
    )
```

```python
import math

import jax
import jax.numpy as jnp
from jax import lax
from jax.experimental import pallas as pl
from jax.experimental.pallas import tpu as pltpu
from jax.sharding import PartitionSpec as P


HEADS = 8
HD = 128
TOPK = 6
BLK = 128
NSEL = 4
HALF = BLK // 2
TOGETHER = 4


def dot_nt(a, b):
    return lax.dot_general(a, b, (((1,), (1,)), ((), ())), preferred_element_type=jnp.float32)


def dot_nn(a, b):
    return lax.dot_general(a, b, (((1,), (0,)), ((), ())), preferred_element_type=jnp.float32)


def dot_tn(a, b):
    return lax.dot_general(a, b, (((0,), (0,)), ((), ())), preferred_element_type=jnp.float32)


def pack_kernel(q_ref, k_ref, v_ref, g_ref, w_ref, out_ref):
    out_grad = dot_nt(g_ref[...], w_ref[...]).astype(jnp.bfloat16)
    for head in range(2):
        cols = slice(head * HD, (head + 1) * HD)
        for half in range(2):
            rows, place = slice(half * HALF, (half + 1) * HALF), 2 * head + half
            out_ref[place, 0:BLK, :] = k_ref[:, cols]
            out_ref[place, BLK : 2 * BLK, :] = v_ref[:, cols]
            out_ref[place, 2 * BLK : 2 * BLK + HALF, :] = q_ref[rows, cols]
            out_ref[place, 2 * BLK + HALF :, :] = out_grad[rows, cols]


def pack_rows(queries, keys, values, grads, out_weight):
    width = out_weight.shape[1]
    col = pl.BlockSpec((BLK, 2 * HD), lambda h: (0, h))
    return pl.pallas_call(
        pack_kernel,
        grid=(HEADS // 2,),
        in_specs=[
            col,
            col,
            col,
            pl.BlockSpec((BLK, width), lambda h: (0, 0)),
            pl.BlockSpec((2 * HD, width), lambda h: (h, 0)),
        ],
        out_specs=pl.BlockSpec((4, 3 * BLK, HD), lambda h: (h, 0, 0)),
        out_shape=jax.ShapeDtypeStruct((2 * HEADS, 3 * BLK, HD), jnp.bfloat16),
        cost_estimate=pl.CostEstimate(
            flops=2 * BLK * HEADS * HD * width, bytes_accessed=7_000_000, transcendentals=0
        ),
        name="pack_rows",
    )(queries, keys, values, grads, out_weight)


def attention_kernel(lists_ref, lengths_ref, half_ref, rows_ref, out_ref, key_acc, value_acc):
    inv_root = 1.0 / math.sqrt(HD)
    blocks = rows_ref.shape[0]
    key_acc[...] = jnp.zeros_like(key_acc)
    value_acc[...] = jnp.zeros_like(value_acc)
    query_at = lax.broadcasted_iota(jnp.int32, (HALF, BLK), 0) + half_ref[0] * HALF
    key_at = lax.broadcasted_iota(jnp.int32, (HALF, BLK), 1)

    def score(i):
        query = rows_ref[i, 2 * BLK : 2 * BLK + HALF, :]
        listed = [lists_ref[i * NSEL + n] for n in range(NSEL)]
        scores = []
        for n, block in enumerate(listed):
            limit = lengths_ref[block]
            for earlier in listed[:n]:
                limit = jnp.where(earlier == block, 0, limit)
            reach = jnp.where(block < i, BLK, 0)
            allowed = (key_at < limit) & (key_at <= query_at + reach)
            raw = dot_nt(query, rows_ref[block, 0:BLK, :]) * inv_root
            scores.append(jnp.where(allowed, raw, -jnp.inf))
        return listed, scores

    def normalize(scores):
        top = scores[0]
        for part in scores[1:]:
            top = jnp.maximum(top, part)
        row_max = jnp.max(top, axis=1, keepdims=True)
        total = jnp.exp(scores[0] - row_max)
        for part in scores[1:]:
            total = total + jnp.exp(part - row_max)
        log_total = row_max + jnp.log(jnp.sum(total, axis=1, keepdims=True))
        return [jnp.exp(part - log_total) for part in scores]

    def terms(i, listed, probs):
        query = rows_ref[i, 2 * BLK : 2 * BLK + HALF, :]
        grad = rows_ref[i, 2 * BLK + HALF :, :]
        lows = [prob.astype(jnp.bfloat16) for prob in probs]
        head = dot_nn(lows[0], rows_ref[listed[0], BLK : 2 * BLK, :])
        for n in range(1, NSEL):
            head = head + dot_nn(lows[n], rows_ref[listed[n], BLK : 2 * BLK, :])
        prob_grads = [dot_nt(grad, rows_ref[block, BLK : 2 * BLK, :]) for block in listed]
        row_delta = jnp.sum(head * grad.astype(jnp.float32), axis=1, keepdims=True)
        dscores = [
            (prob * (prob_grad - row_delta)).astype(jnp.bfloat16)
            for prob, prob_grad in zip(probs, prob_grads)
        ]
        query_sum = dot_nn(dscores[0], rows_ref[listed[0], 0:BLK, :])
        for n in range(1, NSEL):
            query_sum = query_sum + dot_nn(dscores[n], rows_ref[listed[n], 0:BLK, :])
        key_terms = [dot_tn(dscore, query) for dscore in dscores]
        value_terms = [dot_tn(low, grad) for low in lows]
        return query_sum, key_terms, value_terms

    def some_blocks(group, carry):
        rows = [group * TOGETHER + u for u in range(TOGETHER)]
        scored = [score(i) for i in rows]
        probs = [normalize(scores) for _, scores in scored]
        results = [terms(i, scored[u][0], probs[u]) for u, i in enumerate(rows)]
        for u, i in enumerate(rows):
            query_sum, key_terms, value_terms = results[u]
            out_ref[i, 2 * BLK :, :] = (query_sum * inv_root).astype(jnp.bfloat16)
            for n, block in enumerate(scored[u][0]):
                key_acc[block] += key_terms[n]
                value_acc[block] += value_terms[n]
        return carry

    lax.fori_loop(0, blocks // TOGETHER, some_blocks, 0)
    for i in range(blocks):
        out_ref[i, 0:BLK, :] = (key_acc[i] * inv_root).astype(jnp.bfloat16)
        out_ref[i, BLK : 2 * BLK, :] = value_acc[i].astype(jnp.bfloat16)


def attention_rows(lists, lengths, half, rows):
    blocks = rows.shape[0]
    smem = pl.BlockSpec(memory_space=pltpu.SMEM)
    vmem = pl.BlockSpec(memory_space=pltpu.VMEM)
    return pl.pallas_call(
        attention_kernel,
        in_specs=[smem, smem, smem, vmem],
        out_specs=vmem,
        out_shape=jax.ShapeDtypeStruct((blocks, 2 * BLK + HALF, HD), jnp.bfloat16),
        scratch_shapes=[
            pltpu.VMEM((blocks, BLK, HD), jnp.float32),
            pltpu.VMEM((blocks, BLK, HD), jnp.float32),
        ],
        cost_estimate=pl.CostEstimate(flops=0, bytes_accessed=3_000_000, transcendentals=0),
        name="attention_rows",
    )(lists, lengths, half, rows)


def unpack_kernel(rows_ref, query_ref, key_ref, value_ref):
    for h in range(HEADS):
        cols = slice(h * HD, (h + 1) * HD)

        def both(rows):
            first = rows_ref[2 * h, rows, :].astype(jnp.float32)
            return (first + rows_ref[2 * h + 1, rows, :].astype(jnp.float32)).astype(jnp.bfloat16)

        key_ref[:, cols] = both(slice(0, BLK))
        value_ref[:, cols] = both(slice(BLK, 2 * BLK))
        query_ref[0:HALF, cols] = rows_ref[2 * h, 2 * BLK :, :]
        query_ref[HALF:BLK, cols] = rows_ref[2 * h + 1, 2 * BLK :, :]


def unpack_rows(rows):
    vmem = pl.BlockSpec(memory_space=pltpu.VMEM)
    shape = jax.ShapeDtypeStruct((BLK, HEADS * HD), jnp.bfloat16)
    return pl.pallas_call(
        unpack_kernel,
        in_specs=[vmem],
        out_specs=(vmem, vmem, vmem),
        out_shape=(shape, shape, shape),
        cost_estimate=pl.CostEstimate(flops=0, bytes_accessed=2_000_000, transcendentals=0),
        name="unpack_rows",
    )(rows)


def chip_moves(move):
    def index(y, z, core):
        return (y % 4) * 4 + (z % 2) * 2 + core % 2

    return [
        (index(y, z, core), index(*move(y, z, core)))
        for y in range(4)
        for z in range(2)
        for core in range(2)
    ]


Y_UP = chip_moves(lambda y, z, core: (y + 1, z, core))
Y_DOWN = chip_moves(lambda y, z, core: (y - 1, z, core))
Z_SWAP = chip_moves(lambda y, z, core: (y, z + 1, core))
CORE_SWAP = chip_moves(lambda y, z, core: (y, z, core + 1))
PIECE_STEPS = ((0, 0), (0, 1), (-1, 0), (1, 0), (-1, 1), (-2, 0), (1, 1), (2, 1))
LATE = 2


def sequence_moves(move):
    def index(z, x):
        return (z % 2) * 4 + x % 4

    return [(index(z, x), index(*move(z, x))) for z in range(2) for x in range(4)]


X_UP = sequence_moves(lambda z, x: (z, x + 1))
X_DOWN = sequence_moves(lambda z, x: (z, x - 1))
X_FAR = sequence_moves(lambda z, x: (z, x + 2))
X_MOVES = (X_FAR, X_UP, X_DOWN)
FAR_SWAP = sequence_moves(lambda z, x: (z + 1, x))


def pass_on(value, move):
    return lax.ppermute(value, "ctx", move)


def piece_sources(my_index):
    y, z, core = my_index // 4, (my_index // 2) % 2, my_index % 2
    places = []
    for step in range(2):
        for dy, dz in PIECE_STEPS:
            places.append(((y + dy + 4) % 4) * 4 + ((z + dz) % 2) * 2 + (core + step) % 2)
    return jnp.stack(places)


def pick_kernel(count, scaled, *refs):
    onehot_ref, coef_ref = refs[0], refs[1]
    pieces, out_ref = refs[2 : 2 + count], refs[-1]
    slots = onehot_ref.shape[1]
    for p, piece in enumerate(pieces):
        picked = dot_nn(onehot_ref[p], piece[...])
        if scaled:
            picked = picked * coef_ref[p]
        out_ref[p * slots : (p + 1) * slots, :] = picked.astype(jnp.bfloat16)


def pick_rows(onehot, coef, pieces, scaled, buffer, first):
    count, (rows, width), slots = len(pieces), pieces[0].shape, onehot.shape[1]
    tile = 1024
    total = 2 * len(PIECE_STEPS) * slots
    in_specs = [
        pl.BlockSpec((count, slots, rows), lambda j: (0, 0, 0)),
        pl.BlockSpec((count, slots, 1), lambda j: (0, 0, 0)),
    ] + [pl.BlockSpec((rows, tile), lambda j: (0, j))] * count
    operands = [onehot, coef, *pieces]
    aliases = {}
    if buffer is not None:
        aliases = {len(operands): 0}
        operands.append(buffer)
        in_specs.append(pl.BlockSpec(memory_space=pl.ANY))
    block = count * slots
    return pl.pallas_call(
        lambda *refs: pick_kernel(count, scaled, *refs),
        grid=(width // tile,),
        in_specs=in_specs,
        out_specs=pl.BlockSpec((block, tile), lambda j: (first // block, j)),
        out_shape=jax.ShapeDtypeStruct((total, width), jnp.bfloat16),
        input_output_aliases=aliases,
        cost_estimate=pl.CostEstimate(
            flops=2 * block * rows * width,
            bytes_accessed=2 * count * (rows + slots) * width,
            transcendentals=0,
        ),
        name="pick_rows",
    )(*operands)


def route_slots(coef_rows, capacity):
    present = coef_rows > 0.0
    rank = jnp.cumsum(present.astype(jnp.int32), axis=1) - 1
    slot_ids = jnp.arange(capacity, dtype=jnp.int32)
    chosen = present[:, None, :] & (rank[:, None, :] == slot_ids[None, :, None])
    slot_coef = jnp.sum(jnp.where(chosen, coef_rows[:, None, :], 0.0), axis=2, keepdims=True)
    return chosen.astype(jnp.bfloat16), slot_coef


def term_kernel(per_step, homes, order_ref, delta_ref, *refs):
    rows, out_refs = refs[:per_step], refs[per_step:]
    step = pl.program_id(0)
    values = [dot_nn(delta_ref[...], row[...]).astype(jnp.bfloat16) for row in rows]
    for t in range(len(homes) // per_step):

        @pl.when(step == t)
        def _(t=t):
            for u, value in enumerate(values):
                array, place = homes[t * per_step + u]
                out_refs[array][place] = value


def weight_terms(order, delta, rows, stacks):
    count, per_step = order.shape[0], 4
    hidden, slots = delta.shape
    tile = rows.shape[1] // count
    homes = [(a, p) for a, depth in enumerate(stacks) for p in range(depth)]
    return pl.pallas_call(
        lambda *refs: term_kernel(per_step, homes, *refs),
        grid_spec=pltpu.PrefetchScalarGridSpec(
            num_scalar_prefetch=1,
            grid=(count // per_step,),
            in_specs=[pl.BlockSpec((hidden, slots), lambda j, order_ref: (0, 0))]
            + [
                pl.BlockSpec(
                    (slots, tile), lambda j, order_ref, u=u: (0, order_ref[j * per_step + u])
                )
                for u in range(per_step)
            ],
            out_specs=[
                pl.BlockSpec((depth, hidden, tile), lambda j, order_ref: (0, 0, 0))
                for depth in stacks
            ],
        ),
        out_shape=[jax.ShapeDtypeStruct((depth, hidden, tile), jnp.bfloat16) for depth in stacks],
        cost_estimate=pl.CostEstimate(flops=0, bytes_accessed=1_000_000, transcendentals=0),
        name="weight_terms",
    )(order, delta, *([rows] * per_step))


def term_order(steps):
    place = lax.axis_index("dp")
    z, x = place // 4, place % 4
    return jnp.stack([((z + dz) % 2) * 4 + (x + dx) % 4 for dx, dz in steps]).astype(jnp.int32)


X_FIRST = ((2, 0), (2, 1), (1, 0), (1, 1), (3, 0), (3, 1), (0, 0), (0, 1))
Z_FIRST = ((2, 1), (1, 1), (3, 1), (0, 1), (2, 0), (1, 0), (3, 0), (0, 0))


def add_terms(*terms):
    total = terms[0].astype(jnp.float32)
    for term in terms[1:]:
        total = total + term.astype(jnp.float32)
    return total


def sum_x_first(*terms):
    arrived = [lax.ppermute(term, "dp", move) for term, move in zip(terms, X_MOVES)]
    parts = [terms[-1], *arrived]
    across = add_terms(*(part[1] for part in parts)).astype(jnp.bfloat16)
    other = lax.ppermute(across, "dp", FAR_SWAP)
    return add_terms(*(part[0] for part in parts), other).T[None]


def sum_z_first(other, same):
    joined = lax.ppermute(other, "dp", FAR_SWAP)
    sums = [add_terms(same[k], joined[k]).astype(jnp.bfloat16) for k in range(len(X_MOVES))]
    arrived = [lax.ppermute(term, "dp", move) for term, move in zip(sums, X_MOVES)]
    return add_terms(same[-1], joined[-1], *arrived).T[None]


def per_device(
    query_rows,
    key_rows,
    value_rows,
    block_lists,
    block_lengths,
    out_weight,
    expert_input,
    layer_grad,
    route_experts,
    route_weight,
    gate_weight,
    up_weight,
    down_weight,
):
    ctx_count = lax.axis_size("ctx")
    my_index = lax.axis_index("ctx")
    tokens_here = expert_input[0]
    grads_here = layer_grad[0]
    capacity = min(BLK, BLK * TOPK * 4 // (3 * ctx_count))

    all_experts = jnp.arange(ctx_count, dtype=jnp.int32)
    matches = route_experts[0][None, :, :] == all_experts[:, None, None]
    coef_out = jnp.sum(jnp.where(matches, route_weight[0][None], 0.0), axis=2)
    coef_in = lax.all_to_all(coef_out, "ctx", split_axis=0, concat_axis=0, tiled=True)
    keep = len(PIECE_STEPS) - LATE
    early = 2 * keep
    halves = (slice(0, keep), slice(keep + LATE, 2 * keep + LATE))
    tails = (slice(keep, keep + LATE), slice(2 * keep + LATE, None))
    onehot, slot_coef = route_slots(coef_in[piece_sources(my_index)], capacity)
    onehot, slot_coef = (
        jnp.concatenate([v[part] for part in halves + tails]) for v in (onehot, slot_coef)
    )

    def early_pick(mine, others, scaled):
        return pick_rows(onehot[:early], slot_coef[:early], mine + others, scaled, None, 0)

    def late_pick(mine, others, scaled, buffer):
        first = early * capacity
        return pick_rows(onehot[early:], slot_coef[early:], mine + others, scaled, buffer, first)

    beside, below, above = (pass_on(tokens_here, move) for move in (Z_SWAP, Y_UP, Y_DOWN))
    below_beside, far = pass_on(below, Z_SWAP), pass_on(below, Y_UP)
    above_beside = pass_on(beside, Y_DOWN)
    far_beside = pass_on(above_beside, Y_DOWN)
    near_rows = [tokens_here, beside, below, above, below_beside, far]
    near_others = [pass_on(piece, CORE_SWAP) for piece in near_rows]
    far_rows = [above_beside, far_beside]
    far_others = [pass_on(piece, CORE_SWAP) for piece in far_rows]

    packed = pack_rows(query_rows[0], key_rows[0], value_rows[0], grads_here, out_weight)

    g_beside, g_below, g_above = (pass_on(grads_here, move) for move in (Z_SWAP, Y_UP, Y_DOWN))
    g_below_beside, g_far = pass_on(g_below, Z_SWAP), pass_on(g_below, Y_UP)
    g_above_beside = pass_on(g_beside, Y_DOWN)
    g_far_beside = pass_on(g_below_beside, Y_UP)
    buffer = early_pick(near_rows, near_others, False)
    rows_in = late_pick(far_rows, far_others, False, buffer)
    gate_pre = lax.optimization_barrier(dot_nn(rows_in, gate_weight[0]))
    gate_sig = jax.nn.sigmoid(gate_pre)
    gate_act = gate_pre * gate_sig
    up_pre = dot_nn(rows_in, up_weight[0])
    hidden = (gate_act * up_pre).astype(jnp.bfloat16)
    up_pre, hidden = lax.optimization_barrier((up_pre, hidden))
    g_near = [grads_here, g_beside, g_below, g_above, g_below_beside, g_far]
    g_near_others = [pass_on(piece, CORE_SWAP) for piece in g_near]
    g_buffer = early_pick(g_near, g_near_others, True)
    g_fars = [g_above_beside, g_far_beside]
    g_far_others = [pass_on(piece, CORE_SWAP) for piece in g_fars]
    grads_in = late_pick(g_fars, g_far_others, True, g_buffer)

    x_order, z_order = term_order(X_FIRST), term_order(Z_FIRST)
    down_terms = weight_terms(x_order, hidden.T, grads_in, (2, 2, 2, 2))
    down_grad = sum_x_first(*down_terms)
    head_rows = lax.all_to_all(packed, "ctx", split_axis=0, concat_axis=0, tiled=True)
    later_grads = lax.optimization_barrier((grads_in, down_terms[0]))[0]
    hidden_grad = dot_nn(later_grads, down_weight[0])
    gate_delta = (
        hidden_grad * up_pre * gate_sig * (1.0 + gate_pre * (1.0 - gate_sig))
    ).astype(jnp.bfloat16)
    up_delta = (hidden_grad * gate_act).astype(jnp.bfloat16)
    up_grad = sum_z_first(*weight_terms(z_order, up_delta.T, rows_in, (4, 4)))
    gate_terms = weight_terms(x_order, gate_delta.T, rows_in, (2, 2, 2, 2))
    gate_grad = sum_x_first(*gate_terms)

    half = (my_index % 2).astype(jnp.int32).reshape(1)
    grad_rows = attention_rows(block_lists.reshape(-1), block_lengths.reshape(-1), half, head_rows)
    returned = lax.all_to_all(grad_rows, "ctx", split_axis=0, concat_axis=0, tiled=True)
    query_grad, key_grad, value_grad = unpack_rows(returned)
    return (query_grad[None], key_grad[None], value_grad[None], gate_grad, up_grad, down_grad)


def solution(mesh):
    in_specs = (
        P("dp", "ctx", None),
        P("dp", "ctx", None),
        P("dp", "ctx", None),
        P("dp", None, None),
        P("dp", None),
        P(),
        P("dp", "ctx", None),
        P("dp", "ctx", None),
        P("dp", "ctx", None),
        P("dp", "ctx", None),
        P("ctx", None, None),
        P("ctx", None, None),
        P("ctx", None, None),
    )
    out_specs = (
        P("dp", "ctx", None),
        P("dp", "ctx", None),
        P("dp", "ctx", None),
        P("ctx", "dp", None),
        P("ctx", "dp", None),
        P("ctx", "dp", None),
    )
    return jax.shard_map(
        per_device, mesh=mesh, in_specs=in_specs, out_specs=out_specs, check_vma=False
    )
```

```python
import math

import jax
import jax.numpy as jnp
from jax import lax
from jax.experimental import pallas as pl
from jax.experimental.pallas import tpu as pltpu
from jax.sharding import PartitionSpec as P


HEADS = 8
HD = 128
TOPK = 6
BLK = 128
NSEL = 4
HALF = BLK // 2
TOGETHER = 4


def dot_nt(a, b):
    return lax.dot_general(a, b, (((1,), (1,)), ((), ())), preferred_element_type=jnp.float32)


def dot_nn(a, b):
    return lax.dot_general(a, b, (((1,), (0,)), ((), ())), preferred_element_type=jnp.float32)


def dot_tn(a, b):
    return lax.dot_general(a, b, (((0,), (0,)), ((), ())), preferred_element_type=jnp.float32)


def pack_kernel(q_ref, k_ref, v_ref, g_ref, w_ref, out_ref):
    out_grad = dot_nt(g_ref[...], w_ref[...]).astype(jnp.bfloat16)
    for head in range(2):
        cols = slice(head * HD, (head + 1) * HD)
        for half in range(2):
            rows, place = slice(half * HALF, (half + 1) * HALF), 2 * head + half
            out_ref[place, 0:BLK, :] = k_ref[:, cols]
            out_ref[place, BLK : 2 * BLK, :] = v_ref[:, cols]
            out_ref[place, 2 * BLK : 2 * BLK + HALF, :] = q_ref[rows, cols]
            out_ref[place, 2 * BLK + HALF :, :] = out_grad[rows, cols]


def pack_rows(queries, keys, values, grads, out_weight):
    width = out_weight.shape[1]
    col = pl.BlockSpec((BLK, 2 * HD), lambda h: (0, h))
    return pl.pallas_call(
        pack_kernel,
        grid=(HEADS // 2,),
        in_specs=[
            col,
            col,
            col,
            pl.BlockSpec((BLK, width), lambda h: (0, 0)),
            pl.BlockSpec((2 * HD, width), lambda h: (h, 0)),
        ],
        out_specs=pl.BlockSpec((4, 3 * BLK, HD), lambda h: (h, 0, 0)),
        out_shape=jax.ShapeDtypeStruct((2 * HEADS, 3 * BLK, HD), jnp.bfloat16),
        cost_estimate=pl.CostEstimate(
            flops=2 * BLK * HEADS * HD * width, bytes_accessed=7_000_000, transcendentals=0
        ),
        name="pack_rows",
    )(queries, keys, values, grads, out_weight)


def attention_kernel(lists_ref, lengths_ref, half_ref, rows_ref, out_ref, key_acc, value_acc):
    inv_root = 1.0 / math.sqrt(HD)
    blocks = rows_ref.shape[0]
    key_acc[...] = jnp.zeros_like(key_acc)
    value_acc[...] = jnp.zeros_like(value_acc)
    query_at = lax.broadcasted_iota(jnp.int32, (HALF, BLK), 0) + half_ref[0] * HALF
    key_at = lax.broadcasted_iota(jnp.int32, (HALF, BLK), 1)

    def score(i):
        query = rows_ref[i, 2 * BLK : 2 * BLK + HALF, :]
        listed = [lists_ref[i * NSEL + n] for n in range(NSEL)]
        scores = []
        for n, block in enumerate(listed):
            limit = lengths_ref[block]
            for earlier in listed[:n]:
                limit = jnp.where(earlier == block, 0, limit)
            reach = jnp.where(block < i, BLK, 0)
            allowed = (key_at < limit) & (key_at <= query_at + reach)
            raw = dot_nt(query, rows_ref[block, 0:BLK, :]) * inv_root
            scores.append(jnp.where(allowed, raw, -jnp.inf))
        return listed, scores

    def normalize(scores):
        top = scores[0]
        for part in scores[1:]:
            top = jnp.maximum(top, part)
        row_max = jnp.max(top, axis=1, keepdims=True)
        total = jnp.exp(scores[0] - row_max)
        for part in scores[1:]:
            total = total + jnp.exp(part - row_max)
        log_total = row_max + jnp.log(jnp.sum(total, axis=1, keepdims=True))
        return [jnp.exp(part - log_total) for part in scores]

    def terms(i, listed, probs):
        query = rows_ref[i, 2 * BLK : 2 * BLK + HALF, :]
        grad = rows_ref[i, 2 * BLK + HALF :, :]
        lows = [prob.astype(jnp.bfloat16) for prob in probs]
        head = dot_nn(lows[0], rows_ref[listed[0], BLK : 2 * BLK, :])
        for n in range(1, NSEL):
            head = head + dot_nn(lows[n], rows_ref[listed[n], BLK : 2 * BLK, :])
        prob_grads = [dot_nt(grad, rows_ref[block, BLK : 2 * BLK, :]) for block in listed]
        row_delta = jnp.sum(head * grad.astype(jnp.float32), axis=1, keepdims=True)
        dscores = [
            (prob * (prob_grad - row_delta)).astype(jnp.bfloat16)
            for prob, prob_grad in zip(probs, prob_grads)
        ]
        query_sum = dot_nn(dscores[0], rows_ref[listed[0], 0:BLK, :])
        for n in range(1, NSEL):
            query_sum = query_sum + dot_nn(dscores[n], rows_ref[listed[n], 0:BLK, :])
        key_terms = [dot_tn(dscore, query) for dscore in dscores]
        value_terms = [dot_tn(low, grad) for low in lows]
        return query_sum, key_terms, value_terms

    def some_blocks(group, carry):
        rows = [group * TOGETHER + u for u in range(TOGETHER)]
        scored = [score(i) for i in rows]
        probs = [normalize(scores) for _, scores in scored]
        results = [terms(i, scored[u][0], probs[u]) for u, i in enumerate(rows)]
        for u, i in enumerate(rows):
            query_sum, key_terms, value_terms = results[u]
            out_ref[i, 2 * BLK :, :] = (query_sum * inv_root).astype(jnp.bfloat16)
            for n, block in enumerate(scored[u][0]):
                key_acc[block] += key_terms[n]
                value_acc[block] += value_terms[n]
        return carry

    lax.fori_loop(0, blocks // TOGETHER, some_blocks, 0)
    for i in range(blocks):
        out_ref[i, 0:BLK, :] = (key_acc[i] * inv_root).astype(jnp.bfloat16)
        out_ref[i, BLK : 2 * BLK, :] = value_acc[i].astype(jnp.bfloat16)


def attention_rows(lists, lengths, half, rows):
    blocks = rows.shape[0]
    smem = pl.BlockSpec(memory_space=pltpu.SMEM)
    vmem = pl.BlockSpec(memory_space=pltpu.VMEM)
    return pl.pallas_call(
        attention_kernel,
        in_specs=[smem, smem, smem, vmem],
        out_specs=vmem,
        out_shape=jax.ShapeDtypeStruct((blocks, 2 * BLK + HALF, HD), jnp.bfloat16),
        scratch_shapes=[
            pltpu.VMEM((blocks, BLK, HD), jnp.float32),
            pltpu.VMEM((blocks, BLK, HD), jnp.float32),
        ],
        cost_estimate=pl.CostEstimate(flops=0, bytes_accessed=3_000_000, transcendentals=0),
        name="attention_rows",
    )(lists, lengths, half, rows)


def unpack_kernel(rows_ref, query_ref, key_ref, value_ref):
    for h in range(HEADS):
        cols = slice(h * HD, (h + 1) * HD)

        def both(rows):
            first = rows_ref[2 * h, rows, :].astype(jnp.float32)
            return (first + rows_ref[2 * h + 1, rows, :].astype(jnp.float32)).astype(jnp.bfloat16)

        key_ref[:, cols] = both(slice(0, BLK))
        value_ref[:, cols] = both(slice(BLK, 2 * BLK))
        query_ref[0:HALF, cols] = rows_ref[2 * h, 2 * BLK :, :]
        query_ref[HALF:BLK, cols] = rows_ref[2 * h + 1, 2 * BLK :, :]


def unpack_rows(rows):
    vmem = pl.BlockSpec(memory_space=pltpu.VMEM)
    shape = jax.ShapeDtypeStruct((BLK, HEADS * HD), jnp.bfloat16)
    return pl.pallas_call(
        unpack_kernel,
        in_specs=[vmem],
        out_specs=(vmem, vmem, vmem),
        out_shape=(shape, shape, shape),
        cost_estimate=pl.CostEstimate(flops=0, bytes_accessed=2_000_000, transcendentals=0),
        name="unpack_rows",
    )(rows)


def chip_moves(move):
    def index(y, z, core):
        return (y % 4) * 4 + (z % 2) * 2 + core % 2

    return [
        (index(y, z, core), index(*move(y, z, core)))
        for y in range(4)
        for z in range(2)
        for core in range(2)
    ]


Y_UP = chip_moves(lambda y, z, core: (y + 1, z, core))
Y_DOWN = chip_moves(lambda y, z, core: (y - 1, z, core))
Z_SWAP = chip_moves(lambda y, z, core: (y, z + 1, core))
CORE_SWAP = chip_moves(lambda y, z, core: (y, z, core + 1))
PIECE_STEPS = ((0, 0), (0, 1), (-1, 0), (1, 0), (-1, 1), (-2, 0), (1, 1), (2, 1))
LATE = 2


def sequence_moves(move):
    def index(z, x):
        return (z % 2) * 4 + x % 4

    return [(index(z, x), index(*move(z, x))) for z in range(2) for x in range(4)]


X_UP = sequence_moves(lambda z, x: (z, x + 1))
X_DOWN = sequence_moves(lambda z, x: (z, x - 1))
X_FAR = sequence_moves(lambda z, x: (z, x + 2))
X_MOVES = (X_FAR, X_UP, X_DOWN)
FAR_SWAP = sequence_moves(lambda z, x: (z + 1, x))


def pass_on(value, move):
    return lax.ppermute(value, "ctx", move)


def piece_sources(my_index):
    y, z, core = my_index // 4, (my_index // 2) % 2, my_index % 2
    keep = len(PIECE_STEPS) - LATE
    places = []
    for steps in (PIECE_STEPS[:keep], PIECE_STEPS[keep:]):
        for other in range(2):
            for dy, dz in steps:
                places.append(((y + dy + 4) % 4) * 4 + ((z + dz) % 2) * 2 + (core + other) % 2)
    return jnp.stack(places)


def pick_kernel(count, scaled, *refs):
    onehot_ref, coef_ref = refs[0], refs[1]
    pieces, out_ref = refs[2 : 2 + count], refs[-1]
    slots = onehot_ref.shape[1]
    for p, piece in enumerate(pieces):
        picked = dot_nn(onehot_ref[p], piece[...])
        if scaled:
            picked = picked * coef_ref[p]
        out_ref[p * slots : (p + 1) * slots, :] = picked.astype(jnp.bfloat16)


def pick_rows(onehot, coef, pieces, scaled, buffer, first):
    count, (rows, width), slots = len(pieces), pieces[0].shape, onehot.shape[1]
    tile = 1024
    place = first // count
    in_specs = [
        pl.BlockSpec((count, slots, rows), lambda j: (place, 0, 0)),
        pl.BlockSpec((count, slots, 1), lambda j: (place, 0, 0)),
    ] + [pl.BlockSpec((rows, tile), lambda j: (0, j))] * count
    operands = [onehot, coef, *pieces]
    aliases = {}
    if buffer is not None:
        aliases = {len(operands): 0}
        operands.append(buffer)
        in_specs.append(pl.BlockSpec(memory_space=pl.ANY))
    block = count * slots
    return pl.pallas_call(
        lambda *refs: pick_kernel(count, scaled, *refs),
        grid=(width // tile,),
        in_specs=in_specs,
        out_specs=pl.BlockSpec((block, tile), lambda j: (place, j)),
        out_shape=jax.ShapeDtypeStruct((onehot.shape[0] * slots, width), jnp.bfloat16),
        input_output_aliases=aliases,
        cost_estimate=pl.CostEstimate(
            flops=2 * block * rows * width,
            bytes_accessed=2 * count * (rows + slots) * width,
            transcendentals=0,
        ),
        name="pick_rows",
    )(*operands)


def route_slots(coef_rows, capacity):
    present = coef_rows > 0.0
    rank = jnp.cumsum(present.astype(jnp.int32), axis=1) - 1
    slot_ids = jnp.arange(capacity, dtype=jnp.int32)
    chosen = present[:, None, :] & (rank[:, None, :] == slot_ids[None, :, None])
    slot_coef = jnp.sum(jnp.where(chosen, coef_rows[:, None, :], 0.0), axis=2, keepdims=True)
    return chosen.astype(jnp.bfloat16), slot_coef


def term_kernel(per_step, homes, order_ref, delta_ref, *refs):
    rows, out_refs = refs[:per_step], refs[per_step:]
    step = pl.program_id(0)
    values = [dot_nn(delta_ref[...], row[...]).astype(jnp.bfloat16) for row in rows]
    for t in range(len(homes) // per_step):

        @pl.when(step == t)
        def _(t=t):
            for u, value in enumerate(values):
                array, place = homes[t * per_step + u]
                out_refs[array][place] = value


def weight_terms(order, delta, rows, stacks):
    count, per_step = order.shape[0], 4
    hidden, slots = delta.shape
    tile = rows.shape[1] // count
    homes = [(a, p) for a, depth in enumerate(stacks) for p in range(depth)]
    return pl.pallas_call(
        lambda *refs: term_kernel(per_step, homes, *refs),
        grid_spec=pltpu.PrefetchScalarGridSpec(
            num_scalar_prefetch=1,
            grid=(count // per_step,),
            in_specs=[pl.BlockSpec((hidden, slots), lambda j, order_ref: (0, 0))]
            + [
                pl.BlockSpec(
                    (slots, tile), lambda j, order_ref, u=u: (0, order_ref[j * per_step + u])
                )
                for u in range(per_step)
            ],
            out_specs=[
                pl.BlockSpec((depth, hidden, tile), lambda j, order_ref: (0, 0, 0))
                for depth in stacks
            ],
        ),
        out_shape=[jax.ShapeDtypeStruct((depth, hidden, tile), jnp.bfloat16) for depth in stacks],
        cost_estimate=pl.CostEstimate(flops=0, bytes_accessed=1_000_000, transcendentals=0),
        name="weight_terms",
    )(order, delta, *([rows] * per_step))


def term_order(steps):
    place = lax.axis_index("dp")
    z, x = place // 4, place % 4
    return jnp.stack([((z + dz) % 2) * 4 + (x + dx) % 4 for dx, dz in steps]).astype(jnp.int32)


X_FIRST = ((2, 0), (2, 1), (1, 0), (1, 1), (3, 0), (3, 1), (0, 0), (0, 1))
Z_FIRST = ((2, 1), (1, 1), (3, 1), (0, 1), (2, 0), (1, 0), (3, 0), (0, 0))


def add_terms(*terms):
    total = terms[0].astype(jnp.float32)
    for term in terms[1:]:
        total = total + term.astype(jnp.float32)
    return total


def sum_x_first(*terms):
    arrived = [lax.ppermute(term, "dp", move) for term, move in zip(terms, X_MOVES)]
    parts = [terms[-1], *arrived]
    across = add_terms(*(part[1] for part in parts)).astype(jnp.bfloat16)
    other = lax.ppermute(across, "dp", FAR_SWAP)
    return add_terms(*(part[0] for part in parts), other).T[None]


def sum_z_first(other, same):
    joined = lax.ppermute(other, "dp", FAR_SWAP)
    sums = [add_terms(same[k], joined[k]).astype(jnp.bfloat16) for k in range(len(X_MOVES))]
    arrived = [lax.ppermute(term, "dp", move) for term, move in zip(sums, X_MOVES)]
    return add_terms(same[-1], joined[-1], *arrived).T[None]


def per_device(
    query_rows,
    key_rows,
    value_rows,
    block_lists,
    block_lengths,
    out_weight,
    expert_input,
    layer_grad,
    route_experts,
    route_weight,
    gate_weight,
    up_weight,
    down_weight,
):
    ctx_count = lax.axis_size("ctx")
    my_index = lax.axis_index("ctx")
    tokens_here = expert_input[0]
    grads_here = layer_grad[0]
    capacity = min(BLK, BLK * TOPK * 4 // (3 * ctx_count))

    all_experts = jnp.arange(ctx_count, dtype=jnp.int32)
    matches = route_experts[0][None, :, :] == all_experts[:, None, None]
    coef_out = jnp.sum(jnp.where(matches, route_weight[0][None], 0.0), axis=2)
    coef_in = lax.all_to_all(coef_out, "ctx", split_axis=0, concat_axis=0, tiled=True)
    early = 2 * (len(PIECE_STEPS) - LATE)
    onehot, slot_coef = route_slots(coef_in[piece_sources(my_index)], capacity)

    def early_pick(mine, others, scaled):
        return pick_rows(onehot, slot_coef, mine + others, scaled, None, 0)

    def late_pick(mine, others, scaled, buffer):
        return pick_rows(onehot, slot_coef, mine + others, scaled, buffer, early)

    beside, below, above = (pass_on(tokens_here, move) for move in (Z_SWAP, Y_UP, Y_DOWN))
    below_beside, far = pass_on(below, Z_SWAP), pass_on(below, Y_UP)
    above_beside = pass_on(beside, Y_DOWN)
    far_beside = pass_on(above_beside, Y_DOWN)
    near_rows = [tokens_here, beside, below, above, below_beside, far]
    near_others = [pass_on(piece, CORE_SWAP) for piece in near_rows]
    far_rows = [above_beside, far_beside]
    far_others = [pass_on(piece, CORE_SWAP) for piece in far_rows]

    packed = pack_rows(query_rows[0], key_rows[0], value_rows[0], grads_here, out_weight)

    g_beside, g_below, g_above = (pass_on(grads_here, move) for move in (Z_SWAP, Y_UP, Y_DOWN))
    g_below_beside, g_far = pass_on(g_below, Z_SWAP), pass_on(g_below, Y_UP)
    g_above_beside = pass_on(g_beside, Y_DOWN)
    g_far_beside = pass_on(g_below_beside, Y_UP)
    buffer = early_pick(near_rows, near_others, False)
    rows_in = late_pick(far_rows, far_others, False, buffer)
    gate_pre = lax.optimization_barrier(dot_nn(rows_in, gate_weight[0]))
    gate_sig = jax.nn.sigmoid(gate_pre)
    gate_act = gate_pre * gate_sig
    up_pre = dot_nn(rows_in, up_weight[0])
    hidden = (gate_act * up_pre).astype(jnp.bfloat16)
    up_pre, hidden = lax.optimization_barrier((up_pre, hidden))
    g_near = [grads_here, g_beside, g_below, g_above, g_below_beside, g_far]
    g_near_others = [pass_on(piece, CORE_SWAP) for piece in g_near]
    g_buffer = early_pick(g_near, g_near_others, True)
    g_fars = [g_above_beside, g_far_beside]
    g_far_others = [pass_on(piece, CORE_SWAP) for piece in g_fars]
    grads_in = late_pick(g_fars, g_far_others, True, g_buffer)

    x_order, z_order = term_order(X_FIRST), term_order(Z_FIRST)
    down_terms = weight_terms(x_order, hidden.T, grads_in, (2, 2, 2, 2))
    down_grad = sum_x_first(*down_terms)
    head_rows = lax.all_to_all(packed, "ctx", split_axis=0, concat_axis=0, tiled=True)
    later_grads = lax.optimization_barrier((grads_in, down_terms[0]))[0]
    hidden_grad = dot_nn(later_grads, down_weight[0])
    gate_delta = (
        hidden_grad * up_pre * gate_sig * (1.0 + gate_pre * (1.0 - gate_sig))
    ).astype(jnp.bfloat16)
    up_delta = (hidden_grad * gate_act).astype(jnp.bfloat16)
    up_grad = sum_z_first(*weight_terms(z_order, up_delta.T, rows_in, (4, 4)))
    gate_terms = weight_terms(x_order, gate_delta.T, rows_in, (2, 2, 2, 2))
    gate_grad = sum_x_first(*gate_terms)

    half = (my_index % 2).astype(jnp.int32).reshape(1)
    grad_rows = attention_rows(block_lists.reshape(-1), block_lengths.reshape(-1), half, head_rows)
    returned = lax.all_to_all(grad_rows, "ctx", split_axis=0, concat_axis=0, tiled=True)
    query_grad, key_grad, value_grad = unpack_rows(returned)
    return (query_grad[None], key_grad[None], value_grad[None], gate_grad, up_grad, down_grad)


def solution(mesh):
    in_specs = (
        P("dp", "ctx", None),
        P("dp", "ctx", None),
        P("dp", "ctx", None),
        P("dp", None, None),
        P("dp", None),
        P(),
        P("dp", "ctx", None),
        P("dp", "ctx", None),
        P("dp", "ctx", None),
        P("dp", "ctx", None),
        P("ctx", None, None),
        P("ctx", None, None),
        P("ctx", None, None),
    )
    out_specs = (
        P("dp", "ctx", None),
        P("dp", "ctx", None),
        P("dp", "ctx", None),
        P("ctx", "dp", None),
        P("ctx", "dp", None),
        P("ctx", "dp", None),
    )
    return jax.shard_map(
        per_device, mesh=mesh, in_specs=in_specs, out_specs=out_specs, check_vma=False
    )
```

```python
import math

import jax
import jax.numpy as jnp
from jax import lax
from jax.experimental import pallas as pl
from jax.experimental.pallas import tpu as pltpu
from jax.sharding import PartitionSpec as P


HEADS = 8
HD = 128
TOPK = 6
BLK = 128
NSEL = 4
HALF = BLK // 2
TOGETHER = 4


def dot_nt(a, b):
    return lax.dot_general(a, b, (((1,), (1,)), ((), ())), preferred_element_type=jnp.float32)


def dot_nn(a, b):
    return lax.dot_general(a, b, (((1,), (0,)), ((), ())), preferred_element_type=jnp.float32)


def dot_tn(a, b):
    return lax.dot_general(a, b, (((0,), (0,)), ((), ())), preferred_element_type=jnp.float32)


def pack_kernel(q_ref, k_ref, v_ref, g_ref, w_ref, out_ref):
    out_grad = dot_nt(g_ref[...], w_ref[...]).astype(jnp.bfloat16)
    for head in range(2):
        cols = slice(head * HD, (head + 1) * HD)
        for half in range(2):
            rows, place = slice(half * HALF, (half + 1) * HALF), 2 * head + half
            out_ref[place, 0:BLK, :] = k_ref[:, cols]
            out_ref[place, BLK : 2 * BLK, :] = v_ref[:, cols]
            out_ref[place, 2 * BLK : 2 * BLK + HALF, :] = q_ref[rows, cols]
            out_ref[place, 2 * BLK + HALF :, :] = out_grad[rows, cols]


def pack_rows(queries, keys, values, grads, out_weight):
    width = out_weight.shape[1]
    col = pl.BlockSpec((BLK, 2 * HD), lambda h: (0, h))
    return pl.pallas_call(
        pack_kernel,
        grid=(HEADS // 2,),
        in_specs=[
            col,
            col,
            col,
            pl.BlockSpec((BLK, width), lambda h: (0, 0)),
            pl.BlockSpec((2 * HD, width), lambda h: (h, 0)),
        ],
        out_specs=pl.BlockSpec((4, 3 * BLK, HD), lambda h: (h, 0, 0)),
        out_shape=jax.ShapeDtypeStruct((2 * HEADS, 3 * BLK, HD), jnp.bfloat16),
        cost_estimate=pl.CostEstimate(
            flops=2 * BLK * HEADS * HD * width, bytes_accessed=7_000_000, transcendentals=0
        ),
        name="pack_rows",
    )(queries, keys, values, grads, out_weight)


def attention_kernel(lists_ref, lengths_ref, half_ref, rows_ref, out_ref, key_acc, value_acc):
    inv_root = 1.0 / math.sqrt(HD)
    blocks = rows_ref.shape[0]
    key_acc[...] = jnp.zeros_like(key_acc)
    value_acc[...] = jnp.zeros_like(value_acc)
    query_at = lax.broadcasted_iota(jnp.int32, (HALF, BLK), 0) + half_ref[0] * HALF
    key_at = lax.broadcasted_iota(jnp.int32, (HALF, BLK), 1)

    def score(i):
        query = rows_ref[i, 2 * BLK : 2 * BLK + HALF, :]
        listed = [lists_ref[i * NSEL + n] for n in range(NSEL)]
        scores = []
        for n, block in enumerate(listed):
            limit = lengths_ref[block]
            for earlier in listed[:n]:
                limit = jnp.where(earlier == block, 0, limit)
            reach = jnp.where(block < i, BLK, 0)
            allowed = (key_at < limit) & (key_at <= query_at + reach)
            raw = dot_nt(query, rows_ref[block, 0:BLK, :]) * inv_root
            scores.append(jnp.where(allowed, raw, -jnp.inf))
        return listed, scores

    def normalize(scores):
        top = scores[0]
        for part in scores[1:]:
            top = jnp.maximum(top, part)
        row_max = jnp.max(top, axis=1, keepdims=True)
        total = jnp.exp(scores[0] - row_max)
        for part in scores[1:]:
            total = total + jnp.exp(part - row_max)
        log_total = row_max + jnp.log(jnp.sum(total, axis=1, keepdims=True))
        return [jnp.exp(part - log_total) for part in scores]

    def terms(i, listed, probs):
        query = rows_ref[i, 2 * BLK : 2 * BLK + HALF, :]
        grad = rows_ref[i, 2 * BLK + HALF :, :]
        lows = [prob.astype(jnp.bfloat16) for prob in probs]
        head = dot_nn(lows[0], rows_ref[listed[0], BLK : 2 * BLK, :])
        for n in range(1, NSEL):
            head = head + dot_nn(lows[n], rows_ref[listed[n], BLK : 2 * BLK, :])
        prob_grads = [dot_nt(grad, rows_ref[block, BLK : 2 * BLK, :]) for block in listed]
        row_delta = jnp.sum(head * grad.astype(jnp.float32), axis=1, keepdims=True)
        dscores = [
            (prob * (prob_grad - row_delta)).astype(jnp.bfloat16)
            for prob, prob_grad in zip(probs, prob_grads)
        ]
        query_sum = dot_nn(dscores[0], rows_ref[listed[0], 0:BLK, :])
        for n in range(1, NSEL):
            query_sum = query_sum + dot_nn(dscores[n], rows_ref[listed[n], 0:BLK, :])
        key_terms = [dot_tn(dscore, query) for dscore in dscores]
        value_terms = [dot_tn(low, grad) for low in lows]
        return query_sum, key_terms, value_terms

    def some_blocks(group, carry):
        rows = [group * TOGETHER + u for u in range(TOGETHER)]
        scored = [score(i) for i in rows]
        probs = [normalize(scores) for _, scores in scored]
        results = [terms(i, scored[u][0], probs[u]) for u, i in enumerate(rows)]
        for u, i in enumerate(rows):
            query_sum, key_terms, value_terms = results[u]
            out_ref[i, 2 * BLK :, :] = (query_sum * inv_root).astype(jnp.bfloat16)
            for n, block in enumerate(scored[u][0]):
                key_acc[block] += key_terms[n]
                value_acc[block] += value_terms[n]
        return carry

    lax.fori_loop(0, blocks // TOGETHER, some_blocks, 0)
    for i in range(blocks):
        out_ref[i, 0:BLK, :] = (key_acc[i] * inv_root).astype(jnp.bfloat16)
        out_ref[i, BLK : 2 * BLK, :] = value_acc[i].astype(jnp.bfloat16)


def attention_rows(lists, lengths, half, rows):
    blocks = rows.shape[0]
    smem = pl.BlockSpec(memory_space=pltpu.SMEM)
    vmem = pl.BlockSpec(memory_space=pltpu.VMEM)
    return pl.pallas_call(
        attention_kernel,
        in_specs=[smem, smem, smem, vmem],
        out_specs=vmem,
        out_shape=jax.ShapeDtypeStruct((blocks, 2 * BLK + HALF, HD), jnp.bfloat16),
        scratch_shapes=[
            pltpu.VMEM((blocks, BLK, HD), jnp.float32),
            pltpu.VMEM((blocks, BLK, HD), jnp.float32),
        ],
        cost_estimate=pl.CostEstimate(flops=0, bytes_accessed=3_000_000, transcendentals=0),
        name="attention_rows",
    )(lists, lengths, half, rows)


def unpack_kernel(rows_ref, query_ref, key_ref, value_ref):
    for h in range(HEADS):
        cols = slice(h * HD, (h + 1) * HD)

        def both(rows):
            first = rows_ref[2 * h, rows, :].astype(jnp.float32)
            return (first + rows_ref[2 * h + 1, rows, :].astype(jnp.float32)).astype(jnp.bfloat16)

        key_ref[:, cols] = both(slice(0, BLK))
        value_ref[:, cols] = both(slice(BLK, 2 * BLK))
        query_ref[0:HALF, cols] = rows_ref[2 * h, 2 * BLK :, :]
        query_ref[HALF:BLK, cols] = rows_ref[2 * h + 1, 2 * BLK :, :]


def unpack_rows(rows):
    vmem = pl.BlockSpec(memory_space=pltpu.VMEM)
    shape = jax.ShapeDtypeStruct((BLK, HEADS * HD), jnp.bfloat16)
    return pl.pallas_call(
        unpack_kernel,
        in_specs=[vmem],
        out_specs=(vmem, vmem, vmem),
        out_shape=(shape, shape, shape),
        cost_estimate=pl.CostEstimate(flops=0, bytes_accessed=2_000_000, transcendentals=0),
        name="unpack_rows",
    )(rows)


def chip_moves(move):
    def index(y, z, core):
        return (y % 4) * 4 + (z % 2) * 2 + core % 2

    return [
        (index(y, z, core), index(*move(y, z, core)))
        for y in range(4)
        for z in range(2)
        for core in range(2)
    ]


Y_UP = chip_moves(lambda y, z, core: (y + 1, z, core))
Y_DOWN = chip_moves(lambda y, z, core: (y - 1, z, core))
Z_SWAP = chip_moves(lambda y, z, core: (y, z + 1, core))
CORE_SWAP = chip_moves(lambda y, z, core: (y, z, core + 1))
PIECE_STEPS = ((0, 0), (0, 1), (-1, 0), (1, 0), (-1, 1), (-2, 0), (1, 1), (2, 1))
LATE = 2


def sequence_moves(move):
    def index(z, x):
        return (z % 2) * 4 + x % 4

    return [(index(z, x), index(*move(z, x))) for z in range(2) for x in range(4)]


X_UP = sequence_moves(lambda z, x: (z, x + 1))
X_DOWN = sequence_moves(lambda z, x: (z, x - 1))
X_FAR = sequence_moves(lambda z, x: (z, x + 2))
X_MOVES = (X_FAR, X_UP, X_DOWN)
FAR_SWAP = sequence_moves(lambda z, x: (z + 1, x))


def pass_on(value, move):
    return lax.ppermute(value, "ctx", move)


def piece_sources(my_index):
    y, z, core = my_index // 4, (my_index // 2) % 2, my_index % 2
    keep = len(PIECE_STEPS) - LATE
    places = []
    for steps in (PIECE_STEPS[:keep], PIECE_STEPS[keep:]):
        for other in range(2):
            for dy, dz in steps:
                places.append(((y + dy + 4) % 4) * 4 + ((z + dz) % 2) * 2 + (core + other) % 2)
    return jnp.stack(places)


def pick_kernel(count, scaled, *refs):
    onehot_ref, coef_ref = refs[0], refs[1]
    pieces, out_ref = refs[2 : 2 + count], refs[-1]
    slots = onehot_ref.shape[1]
    for p, piece in enumerate(pieces):
        picked = dot_nn(onehot_ref[p], piece[...])
        if scaled:
            picked = picked * coef_ref[p]
        out_ref[p * slots : (p + 1) * slots, :] = picked.astype(jnp.bfloat16)


def pick_rows(onehot, coef, pieces, scaled, buffer, first):
    count, (rows, width), slots = len(pieces), pieces[0].shape, onehot.shape[1]
    tile = 1024
    place = first // count
    in_specs = [
        pl.BlockSpec((count, slots, rows), lambda j: (place, 0, 0)),
        pl.BlockSpec((count, slots, 1), lambda j: (place, 0, 0)),
    ] + [pl.BlockSpec((rows, tile), lambda j: (0, j))] * count
    operands = [onehot, coef, *pieces]
    aliases = {}
    if buffer is not None:
        aliases = {len(operands): 0}
        operands.append(buffer)
        in_specs.append(pl.BlockSpec(memory_space=pl.ANY))
    block = count * slots
    return pl.pallas_call(
        lambda *refs: pick_kernel(count, scaled, *refs),
        grid=(width // tile,),
        in_specs=in_specs,
        out_specs=pl.BlockSpec((block, tile), lambda j: (place, j)),
        out_shape=jax.ShapeDtypeStruct((onehot.shape[0] * slots, width), jnp.bfloat16),
        input_output_aliases=aliases,
        cost_estimate=pl.CostEstimate(
            flops=2 * block * rows * width,
            bytes_accessed=2 * count * (rows + slots) * width,
            transcendentals=0,
        ),
        name="pick_rows",
    )(*operands)


def route_slots(coef_rows, capacity):
    present = coef_rows > 0.0
    rank = jnp.cumsum(present.astype(jnp.int32), axis=1) - 1
    slot_ids = jnp.arange(capacity, dtype=jnp.int32)
    chosen = present[:, None, :] & (rank[:, None, :] == slot_ids[None, :, None])
    slot_coef = jnp.sum(jnp.where(chosen, coef_rows[:, None, :], 0.0), axis=2, keepdims=True)
    return chosen.astype(jnp.bfloat16), slot_coef


def term_kernel(per_step, homes, order_ref, delta_ref, *refs):
    rows, out_refs = refs[:per_step], refs[per_step:]
    step = pl.program_id(0)
    values = [dot_nn(delta_ref[...], row[...]).astype(jnp.bfloat16) for row in rows]
    for t in range(len(homes) // per_step):

        @pl.when(step == t)
        def _(t=t):
            for u, value in enumerate(values):
                array, place = homes[t * per_step + u]
                out_refs[array][place] = value


def weight_terms(order, delta, rows, stacks):
    count, per_step = order.shape[0], 4
    hidden, slots = delta.shape
    tile = rows.shape[1] // count
    homes = [(a, p) for a, depth in enumerate(stacks) for p in range(depth)]
    return pl.pallas_call(
        lambda *refs: term_kernel(per_step, homes, *refs),
        grid_spec=pltpu.PrefetchScalarGridSpec(
            num_scalar_prefetch=1,
            grid=(count // per_step,),
            in_specs=[pl.BlockSpec((hidden, slots), lambda j, order_ref: (0, 0))]
            + [
                pl.BlockSpec(
                    (slots, tile), lambda j, order_ref, u=u: (0, order_ref[j * per_step + u])
                )
                for u in range(per_step)
            ],
            out_specs=[
                pl.BlockSpec((depth, hidden, tile), lambda j, order_ref: (0, 0, 0))
                for depth in stacks
            ],
        ),
        out_shape=[jax.ShapeDtypeStruct((depth, hidden, tile), jnp.bfloat16) for depth in stacks],
        cost_estimate=pl.CostEstimate(flops=0, bytes_accessed=1_000_000, transcendentals=0),
        name="weight_terms",
    )(order, delta, *([rows] * per_step))


def term_order(steps):
    place = lax.axis_index("dp")
    z, x = place // 4, place % 4
    return jnp.stack([((z + dz) % 2) * 4 + (x + dx) % 4 for dx, dz in steps]).astype(jnp.int32)


X_FIRST = ((2, 0), (2, 1), (1, 0), (1, 1), (3, 0), (3, 1), (0, 0), (0, 1))
Z_FIRST = ((2, 1), (1, 1), (3, 1), (0, 1), (2, 0), (1, 0), (3, 0), (0, 0))


def add_terms(*terms):
    total = terms[0].astype(jnp.float32)
    for term in terms[1:]:
        total = total + term.astype(jnp.float32)
    return total


def sum_x_first(*terms):
    arrived = [lax.ppermute(term, "dp", move) for term, move in zip(terms, X_MOVES)]
    parts = [terms[-1], *arrived]
    across = add_terms(*(part[1] for part in parts)).astype(jnp.bfloat16)
    other = lax.ppermute(across, "dp", FAR_SWAP)
    return add_terms(*(part[0] for part in parts), other).T[None]


def sum_z_first(other, same):
    joined = lax.ppermute(other, "dp", FAR_SWAP)
    sums = [add_terms(same[k], joined[k]).astype(jnp.bfloat16) for k in range(len(X_MOVES))]
    arrived = [lax.ppermute(term, "dp", move) for term, move in zip(sums, X_MOVES)]
    return add_terms(same[-1], joined[-1], *arrived).T[None]


def per_device(
    query_rows,
    key_rows,
    value_rows,
    block_lists,
    block_lengths,
    out_weight,
    expert_input,
    layer_grad,
    route_experts,
    route_weight,
    gate_weight,
    up_weight,
    down_weight,
):
    ctx_count = lax.axis_size("ctx")
    my_index = lax.axis_index("ctx")
    tokens_here = expert_input[0]
    grads_here = layer_grad[0]
    capacity = min(BLK, BLK * TOPK * 4 // (3 * ctx_count))

    all_experts = jnp.arange(ctx_count, dtype=jnp.int32)
    matches = route_experts[0][None, :, :] == all_experts[:, None, None]
    coef_out = jnp.sum(jnp.where(matches, route_weight[0][None], 0.0), axis=2)
    coef_in = lax.all_to_all(coef_out, "ctx", split_axis=0, concat_axis=0, tiled=True)
    early = 2 * (len(PIECE_STEPS) - LATE)
    onehot, slot_coef = route_slots(coef_in[piece_sources(my_index)], capacity)

    def early_pick(mine, others, scaled):
        return pick_rows(onehot, slot_coef, mine + others, scaled, None, 0)

    def late_pick(mine, others, scaled, buffer):
        return pick_rows(onehot, slot_coef, mine + others, scaled, buffer, early)

    beside, below, above = (pass_on(tokens_here, move) for move in (Z_SWAP, Y_UP, Y_DOWN))
    below_beside, far = pass_on(below, Z_SWAP), pass_on(below, Y_UP)
    above_beside = pass_on(beside, Y_DOWN)
    far_beside = pass_on(above_beside, Y_DOWN)
    near_rows = [tokens_here, beside, below, above, below_beside, far]
    near_others = [pass_on(piece, CORE_SWAP) for piece in near_rows]
    far_rows = [above_beside, far_beside]
    far_others = [pass_on(piece, CORE_SWAP) for piece in far_rows]

    packed = pack_rows(query_rows[0], key_rows[0], value_rows[0], grads_here, out_weight)

    g_beside, g_below, g_above = (pass_on(grads_here, move) for move in (Z_SWAP, Y_UP, Y_DOWN))
    g_below_beside, g_far = pass_on(g_below, Z_SWAP), pass_on(g_below, Y_UP)
    g_above_beside = pass_on(g_beside, Y_DOWN)
    g_far_beside = pass_on(g_below_beside, Y_UP)
    buffer = early_pick(near_rows, near_others, False)
    rows_in = late_pick(far_rows, far_others, False, buffer)
    gate_pre = lax.optimization_barrier(dot_nn(rows_in, gate_weight[0]))
    up_pre = dot_nn(rows_in, up_weight[0])
    gate_sig = jax.nn.sigmoid(gate_pre)
    gate_act = gate_pre * gate_sig
    hidden = (gate_act * up_pre).astype(jnp.bfloat16)
    gate_slope = up_pre * gate_sig * (1.0 + gate_pre * (1.0 - gate_sig))
    hidden, gate_act, gate_slope = lax.optimization_barrier((hidden, gate_act, gate_slope))
    g_near = [grads_here, g_beside, g_below, g_above, g_below_beside, g_far]
    g_near_others = [pass_on(piece, CORE_SWAP) for piece in g_near]
    g_buffer = early_pick(g_near, g_near_others, True)
    g_fars = [g_above_beside, g_far_beside]
    g_far_others = [pass_on(piece, CORE_SWAP) for piece in g_fars]
    grads_in = late_pick(g_fars, g_far_others, True, g_buffer)

    x_order, z_order = term_order(X_FIRST), term_order(Z_FIRST)
    down_terms = weight_terms(x_order, hidden.T, grads_in, (2, 2, 2, 2))
    down_grad = sum_x_first(*down_terms)
    head_rows = lax.all_to_all(packed, "ctx", split_axis=0, concat_axis=0, tiled=True)
    later_grads = lax.optimization_barrier((grads_in, down_terms[0]))[0]
    hidden_grad = dot_nn(later_grads, down_weight[0])
    gate_delta = (hidden_grad * gate_slope).astype(jnp.bfloat16)
    up_delta = (hidden_grad * gate_act).astype(jnp.bfloat16)
    up_grad = sum_z_first(*weight_terms(z_order, up_delta.T, rows_in, (4, 4)))
    gate_terms = weight_terms(x_order, gate_delta.T, rows_in, (2, 2, 2, 2))
    gate_grad = sum_x_first(*gate_terms)

    half = (my_index % 2).astype(jnp.int32).reshape(1)
    grad_rows = attention_rows(block_lists.reshape(-1), block_lengths.reshape(-1), half, head_rows)
    returned = lax.all_to_all(grad_rows, "ctx", split_axis=0, concat_axis=0, tiled=True)
    query_grad, key_grad, value_grad = unpack_rows(returned)
    return (query_grad[None], key_grad[None], value_grad[None], gate_grad, up_grad, down_grad)


def solution(mesh):
    in_specs = (
        P("dp", "ctx", None),
        P("dp", "ctx", None),
        P("dp", "ctx", None),
        P("dp", None, None),
        P("dp", None),
        P(),
        P("dp", "ctx", None),
        P("dp", "ctx", None),
        P("dp", "ctx", None),
        P("dp", "ctx", None),
        P("ctx", None, None),
        P("ctx", None, None),
        P("ctx", None, None),
    )
    out_specs = (
        P("dp", "ctx", None),
        P("dp", "ctx", None),
        P("dp", "ctx", None),
        P("ctx", "dp", None),
        P("ctx", "dp", None),
        P("ctx", "dp", None),
    )
    return jax.shard_map(
        per_device, mesh=mesh, in_specs=in_specs, out_specs=out_specs, check_vma=False
    )
```

```python
import math

import jax
import jax.numpy as jnp
from jax import lax
from jax.experimental import pallas as pl
from jax.experimental.pallas import tpu as pltpu
from jax.sharding import PartitionSpec as P


HEADS = 8
HD = 128
TOPK = 6
BLK = 128
NSEL = 4
HALF = BLK // 2
TOGETHER = 4


def dot_nt(a, b):
    return lax.dot_general(a, b, (((1,), (1,)), ((), ())), preferred_element_type=jnp.float32)


def dot_nn(a, b):
    return lax.dot_general(a, b, (((1,), (0,)), ((), ())), preferred_element_type=jnp.float32)


def dot_tn(a, b):
    return lax.dot_general(a, b, (((0,), (0,)), ((), ())), preferred_element_type=jnp.float32)


def pack_kernel(q_ref, k_ref, v_ref, g_ref, w_ref, out_ref):
    out_grad = dot_nt(g_ref[...], w_ref[...]).astype(jnp.bfloat16)
    for head in range(2):
        cols = slice(head * HD, (head + 1) * HD)
        for half in range(2):
            rows, place = slice(half * HALF, (half + 1) * HALF), 2 * head + half
            out_ref[place, 0:BLK, :] = k_ref[:, cols]
            out_ref[place, BLK : 2 * BLK, :] = v_ref[:, cols]
            out_ref[place, 2 * BLK : 2 * BLK + HALF, :] = q_ref[rows, cols]
            out_ref[place, 2 * BLK + HALF :, :] = out_grad[rows, cols]


def pack_rows(queries, keys, values, grads, out_weight):
    width = out_weight.shape[1]
    col = pl.BlockSpec((BLK, 2 * HD), lambda h: (0, h))
    return pl.pallas_call(
        pack_kernel,
        grid=(HEADS // 2,),
        in_specs=[
            col,
            col,
            col,
            pl.BlockSpec((BLK, width), lambda h: (0, 0)),
            pl.BlockSpec((2 * HD, width), lambda h: (h, 0)),
        ],
        out_specs=pl.BlockSpec((4, 3 * BLK, HD), lambda h: (h, 0, 0)),
        out_shape=jax.ShapeDtypeStruct((2 * HEADS, 3 * BLK, HD), jnp.bfloat16),
        cost_estimate=pl.CostEstimate(
            flops=2 * BLK * HEADS * HD * width, bytes_accessed=7_000_000, transcendentals=0
        ),
        name="pack_rows",
    )(queries, keys, values, grads, out_weight)


def attention_kernel(
    lists_ref, lengths_ref, half_ref, rows_ref, out_ref, give_ref, key_acc, value_acc
):
    inv_root = 1.0 / math.sqrt(HD)
    blocks = rows_ref.shape[0]
    key_acc[...] = jnp.zeros_like(key_acc)
    value_acc[...] = jnp.zeros_like(value_acc)
    query_at = lax.broadcasted_iota(jnp.int32, (HALF, BLK), 0) + half_ref[0] * HALF
    key_at = lax.broadcasted_iota(jnp.int32, (HALF, BLK), 1)

    def score(i):
        query = rows_ref[i, 2 * BLK : 2 * BLK + HALF, :]
        listed = [lists_ref[i * NSEL + n] for n in range(NSEL)]
        scores = []
        for n, block in enumerate(listed):
            limit = lengths_ref[block]
            for earlier in listed[:n]:
                limit = jnp.where(earlier == block, 0, limit)
            reach = jnp.where(block < i, BLK, 0)
            allowed = (key_at < limit) & (key_at <= query_at + reach)
            raw = dot_nt(query, rows_ref[block, 0:BLK, :]) * inv_root
            scores.append(jnp.where(allowed, raw, -jnp.inf))
        return listed, scores

    def normalize(scores):
        top = scores[0]
        for part in scores[1:]:
            top = jnp.maximum(top, part)
        row_max = jnp.max(top, axis=1, keepdims=True)
        total = jnp.exp(scores[0] - row_max)
        for part in scores[1:]:
            total = total + jnp.exp(part - row_max)
        log_total = row_max + jnp.log(jnp.sum(total, axis=1, keepdims=True))
        return [jnp.exp(part - log_total) for part in scores]

    def terms(i, listed, probs):
        query = rows_ref[i, 2 * BLK : 2 * BLK + HALF, :]
        grad = rows_ref[i, 2 * BLK + HALF :, :]
        lows = [prob.astype(jnp.bfloat16) for prob in probs]
        head = dot_nn(lows[0], rows_ref[listed[0], BLK : 2 * BLK, :])
        for n in range(1, NSEL):
            head = head + dot_nn(lows[n], rows_ref[listed[n], BLK : 2 * BLK, :])
        prob_grads = [dot_nt(grad, rows_ref[block, BLK : 2 * BLK, :]) for block in listed]
        row_delta = jnp.sum(head * grad.astype(jnp.float32), axis=1, keepdims=True)
        dscores = [
            (prob * (prob_grad - row_delta)).astype(jnp.bfloat16)
            for prob, prob_grad in zip(probs, prob_grads)
        ]
        query_sum = dot_nn(dscores[0], rows_ref[listed[0], 0:BLK, :])
        for n in range(1, NSEL):
            query_sum = query_sum + dot_nn(dscores[n], rows_ref[listed[n], 0:BLK, :])
        key_terms = [dot_tn(dscore, query) for dscore in dscores]
        value_terms = [dot_tn(low, grad) for low in lows]
        return query_sum, key_terms, value_terms

    def some_blocks(group, carry):
        rows = [group * TOGETHER + u for u in range(TOGETHER)]
        scored = [score(i) for i in rows]
        probs = [normalize(scores) for _, scores in scored]
        results = [terms(i, scored[u][0], probs[u]) for u, i in enumerate(rows)]
        for u, i in enumerate(rows):
            query_sum, key_terms, value_terms = results[u]
            out_ref[i, BLK:, :] = (query_sum * inv_root).astype(jnp.bfloat16)
            for n, block in enumerate(scored[u][0]):
                key_acc[block] += key_terms[n]
                value_acc[block] += value_terms[n]
        return carry

    lax.fori_loop(0, blocks // TOGETHER, some_blocks, 0)
    for ref, half in ((out_ref, half_ref[0]), (give_ref, 1 - half_ref[0])):
        rows = pl.ds(pl.multiple_of(half * HALF, HALF), HALF)
        for i in range(blocks):
            ref[i, 0:HALF, :] = (key_acc[i, rows, :] * inv_root).astype(jnp.bfloat16)
            ref[i, HALF:BLK, :] = value_acc[i, rows, :].astype(jnp.bfloat16)


def attention_rows(lists, lengths, half, rows):
    blocks = rows.shape[0]
    smem = pl.BlockSpec(memory_space=pltpu.SMEM)
    vmem = pl.BlockSpec(memory_space=pltpu.VMEM)
    return pl.pallas_call(
        attention_kernel,
        in_specs=[smem, smem, smem, vmem],
        out_specs=(vmem, vmem),
        out_shape=(
            jax.ShapeDtypeStruct((blocks, BLK + HALF, HD), jnp.bfloat16),
            jax.ShapeDtypeStruct((blocks, BLK, HD), jnp.bfloat16),
        ),
        scratch_shapes=[
            pltpu.VMEM((blocks, BLK, HD), jnp.float32),
            pltpu.VMEM((blocks, BLK, HD), jnp.float32),
        ],
        cost_estimate=pl.CostEstimate(flops=0, bytes_accessed=3_000_000, transcendentals=0),
        name="attention_rows",
    )(lists, lengths, half, rows)


def unpack_kernel(rows_ref, query_ref, key_ref, value_ref):
    for place in range(2 * HEADS):
        head, half = place // 2, place % 2
        cols, rows = slice(head * HD, (head + 1) * HD), slice(half * HALF, (half + 1) * HALF)
        for k, ref in enumerate((key_ref, value_ref, query_ref)):
            ref[rows, cols] = rows_ref[place, k * HALF : (k + 1) * HALF, :]


def unpack_rows(rows):
    vmem = pl.BlockSpec(memory_space=pltpu.VMEM)
    shape = jax.ShapeDtypeStruct((BLK, HEADS * HD), jnp.bfloat16)
    return pl.pallas_call(
        unpack_kernel,
        in_specs=[vmem],
        out_specs=(vmem, vmem, vmem),
        out_shape=(shape, shape, shape),
        cost_estimate=pl.CostEstimate(flops=0, bytes_accessed=2_000_000, transcendentals=0),
        name="unpack_rows",
    )(rows)


def chip_moves(move):
    def index(y, z, core):
        return (y % 4) * 4 + (z % 2) * 2 + core % 2

    return [
        (index(y, z, core), index(*move(y, z, core)))
        for y in range(4)
        for z in range(2)
        for core in range(2)
    ]


Y_UP = chip_moves(lambda y, z, core: (y + 1, z, core))
Y_DOWN = chip_moves(lambda y, z, core: (y - 1, z, core))
Z_SWAP = chip_moves(lambda y, z, core: (y, z + 1, core))
CORE_SWAP = chip_moves(lambda y, z, core: (y, z, core + 1))
PIECE_STEPS = ((0, 0), (0, 1), (-1, 0), (1, 0), (-1, 1), (-2, 0), (1, 1), (2, 1))
LATE = 2


def sequence_moves(move):
    def index(z, x):
        return (z % 2) * 4 + x % 4

    return [(index(z, x), index(*move(z, x))) for z in range(2) for x in range(4)]


X_UP = sequence_moves(lambda z, x: (z, x + 1))
X_DOWN = sequence_moves(lambda z, x: (z, x - 1))
X_FAR = sequence_moves(lambda z, x: (z, x + 2))
X_MOVES = (X_FAR, X_UP, X_DOWN)
FAR_SWAP = sequence_moves(lambda z, x: (z + 1, x))


def pass_on(value, move):
    return lax.ppermute(value, "ctx", move)


def piece_sources(my_index):
    y, z, core = my_index // 4, (my_index // 2) % 2, my_index % 2
    keep = len(PIECE_STEPS) - LATE
    places = []
    for steps in (PIECE_STEPS[:keep], PIECE_STEPS[keep:]):
        for other in range(2):
            for dy, dz in steps:
                places.append(((y + dy + 4) % 4) * 4 + ((z + dz) % 2) * 2 + (core + other) % 2)
    return jnp.stack(places)


def pick_kernel(count, scaled, *refs):
    onehot_ref, coef_ref = refs[0], refs[1]
    pieces, out_ref = refs[2 : 2 + count], refs[-1]
    slots = onehot_ref.shape[1]
    for p, piece in enumerate(pieces):
        picked = dot_nn(onehot_ref[p], piece[...])
        if scaled:
            picked = picked * coef_ref[p]
        out_ref[p * slots : (p + 1) * slots, :] = picked.astype(jnp.bfloat16)


def pick_rows(onehot, coef, pieces, scaled, buffer, first):
    count, (rows, width), slots = len(pieces), pieces[0].shape, onehot.shape[1]
    tile = 1024
    place = first // count
    in_specs = [
        pl.BlockSpec((count, slots, rows), lambda j: (place, 0, 0)),
        pl.BlockSpec((count, slots, 1), lambda j: (place, 0, 0)),
    ] + [pl.BlockSpec((rows, tile), lambda j: (0, j))] * count
    operands = [onehot, coef, *pieces]
    aliases = {}
    if buffer is not None:
        aliases = {len(operands): 0}
        operands.append(buffer)
        in_specs.append(pl.BlockSpec(memory_space=pl.ANY))
    block = count * slots
    return pl.pallas_call(
        lambda *refs: pick_kernel(count, scaled, *refs),
        grid=(width // tile,),
        in_specs=in_specs,
        out_specs=pl.BlockSpec((block, tile), lambda j: (place, j)),
        out_shape=jax.ShapeDtypeStruct((onehot.shape[0] * slots, width), jnp.bfloat16),
        input_output_aliases=aliases,
        cost_estimate=pl.CostEstimate(
            flops=2 * block * rows * width,
            bytes_accessed=2 * count * (rows + slots) * width,
            transcendentals=0,
        ),
        name="pick_rows",
    )(*operands)


def route_slots(coef_rows, capacity):
    present = coef_rows > 0.0
    rank = jnp.cumsum(present.astype(jnp.int32), axis=1) - 1
    slot_ids = jnp.arange(capacity, dtype=jnp.int32)
    chosen = present[:, None, :] & (rank[:, None, :] == slot_ids[None, :, None])
    slot_coef = jnp.sum(jnp.where(chosen, coef_rows[:, None, :], 0.0), axis=2, keepdims=True)
    return chosen.astype(jnp.bfloat16), slot_coef


def term_kernel(per_step, order_ref, delta_ref, *refs):
    rows, out_refs = refs[:per_step], refs[per_step:]
    depth = per_step // len(out_refs)
    for u, row in enumerate(rows):
        out_refs[u // depth][u % depth] = dot_nn(delta_ref[...], row[...]).astype(jnp.bfloat16)


def weight_terms(order, delta, rows, arrays):
    count, per_step = order.shape[0], 4
    hidden, slots = delta.shape
    tile = rows.shape[1] // count
    depth = per_step // arrays
    shape = jax.ShapeDtypeStruct((count // arrays, hidden, tile), jnp.bfloat16)
    return pl.pallas_call(
        lambda *refs: term_kernel(per_step, *refs),
        grid_spec=pltpu.PrefetchScalarGridSpec(
            num_scalar_prefetch=1,
            grid=(count // per_step,),
            in_specs=[pl.BlockSpec((hidden, slots), lambda j, order_ref: (0, 0))]
            + [
                pl.BlockSpec(
                    (slots, tile), lambda j, order_ref, u=u: (0, order_ref[j * per_step + u])
                )
                for u in range(per_step)
            ],
            out_specs=[pl.BlockSpec((depth, hidden, tile), lambda j, order_ref: (j, 0, 0))] * arrays,
        ),
        out_shape=[shape] * arrays,
        cost_estimate=pl.CostEstimate(flops=0, bytes_accessed=1_000_000, transcendentals=0),
        name="weight_terms",
    )(order, delta, *([rows] * per_step))


def term_order(steps):
    place = lax.axis_index("dp")
    z, x = place // 4, place % 4
    return jnp.stack([((z + dz) % 2) * 4 + (x + dx) % 4 for dx, dz in steps]).astype(jnp.int32)


X_FIRST = ((2, 0), (1, 0), (3, 0), (0, 0), (2, 1), (1, 1), (3, 1), (0, 1))
Z_FIRST = ((2, 1), (1, 1), (2, 0), (1, 0), (3, 1), (0, 1), (3, 0), (0, 0))


def add_terms(*terms):
    total = terms[0].astype(jnp.float32)
    for term in terms[1:]:
        total = total + term.astype(jnp.float32)
    return total


def sum_x_first(*terms):
    arrived = [lax.ppermute(term, "dp", move) for term, move in zip(terms, X_MOVES)]
    parts = [terms[-1], *arrived]
    across = add_terms(*(part[1] for part in parts)).astype(jnp.bfloat16)
    other = lax.ppermute(across, "dp", FAR_SWAP)
    return add_terms(*(part[0] for part in parts), other).T[None]


def sum_z_first(other, same):
    joined = lax.ppermute(other, "dp", FAR_SWAP)
    sums = [add_terms(same[k], joined[k]).astype(jnp.bfloat16) for k in range(len(X_MOVES))]
    arrived = [lax.ppermute(term, "dp", move) for term, move in zip(sums, X_MOVES)]
    return add_terms(same[-1], joined[-1], *arrived).T[None]


def per_device(
    query_rows,
    key_rows,
    value_rows,
    block_lists,
    block_lengths,
    out_weight,
    expert_input,
    layer_grad,
    route_experts,
    route_weight,
    gate_weight,
    up_weight,
    down_weight,
):
    ctx_count = lax.axis_size("ctx")
    my_index = lax.axis_index("ctx")
    tokens_here = expert_input[0]
    grads_here = layer_grad[0]
    capacity = min(BLK, BLK * TOPK * 4 // (3 * ctx_count))

    all_experts = jnp.arange(ctx_count, dtype=jnp.int32)
    matches = route_experts[0][None, :, :] == all_experts[:, None, None]
    coef_out = jnp.sum(jnp.where(matches, route_weight[0][None], 0.0), axis=2)
    coef_in = lax.all_to_all(coef_out, "ctx", split_axis=0, concat_axis=0, tiled=True)
    early = 2 * (len(PIECE_STEPS) - LATE)
    onehot, slot_coef = route_slots(coef_in[piece_sources(my_index)], capacity)

    def early_pick(mine, others, scaled):
        return pick_rows(onehot, slot_coef, mine + others, scaled, None, 0)

    def late_pick(mine, others, scaled, buffer):
        return pick_rows(onehot, slot_coef, mine + others, scaled, buffer, early)

    beside, below, above = (pass_on(tokens_here, move) for move in (Z_SWAP, Y_UP, Y_DOWN))
    below_beside, far = pass_on(below, Z_SWAP), pass_on(below, Y_UP)
    above_beside = pass_on(beside, Y_DOWN)
    far_beside = pass_on(above_beside, Y_DOWN)
    near_rows = [tokens_here, beside, below, above, below_beside, far]
    near_others = [pass_on(piece, CORE_SWAP) for piece in near_rows]
    far_rows = [above_beside, far_beside]
    far_others = [pass_on(piece, CORE_SWAP) for piece in far_rows]

    packed = pack_rows(query_rows[0], key_rows[0], value_rows[0], grads_here, out_weight)

    g_beside, g_below, g_above = (pass_on(grads_here, move) for move in (Z_SWAP, Y_UP, Y_DOWN))
    g_below_beside, g_far = pass_on(g_below, Z_SWAP), pass_on(g_below, Y_UP)
    g_above_beside = pass_on(g_beside, Y_DOWN)
    g_far_beside = pass_on(g_below_beside, Y_UP)
    buffer = early_pick(near_rows, near_others, False)
    rows_in = late_pick(far_rows, far_others, False, buffer)
    gate_pre = lax.optimization_barrier(dot_nn(rows_in, gate_weight[0]))
    up_pre = dot_nn(rows_in, up_weight[0])
    gate_sig = jax.nn.sigmoid(gate_pre)
    gate_act = gate_pre * gate_sig
    hidden = (gate_act * up_pre).astype(jnp.bfloat16)
    gate_slope = up_pre * gate_sig * (1.0 + gate_pre * (1.0 - gate_sig))
    hidden, gate_act, gate_slope = lax.optimization_barrier((hidden, gate_act, gate_slope))
    g_near = [grads_here, g_beside, g_below, g_above, g_below_beside, g_far]
    g_near_others = [pass_on(piece, CORE_SWAP) for piece in g_near]
    g_buffer = early_pick(g_near, g_near_others, True)
    g_fars = [g_above_beside, g_far_beside]
    g_far_others = [pass_on(piece, CORE_SWAP) for piece in g_fars]
    grads_in = late_pick(g_fars, g_far_others, True, g_buffer)

    x_order, z_order = term_order(X_FIRST), term_order(Z_FIRST)
    down_terms = weight_terms(x_order, hidden.T, grads_in, 4)
    down_grad = sum_x_first(*down_terms)
    head_rows = lax.all_to_all(packed, "ctx", split_axis=0, concat_axis=0, tiled=True)
    later_grads = lax.optimization_barrier((grads_in, down_terms[0]))[0]
    hidden_grad = dot_nn(later_grads, down_weight[0])
    gate_delta = (hidden_grad * gate_slope).astype(jnp.bfloat16)
    up_delta = (hidden_grad * gate_act).astype(jnp.bfloat16)
    up_grad = sum_z_first(*weight_terms(z_order, up_delta.T, rows_in, 2))
    gate_terms = weight_terms(x_order, gate_delta.T, rows_in, 4)
    gate_grad = sum_x_first(*gate_terms)

    half = (my_index % 2).astype(jnp.int32).reshape(1)
    kept, given = attention_rows(
        block_lists.reshape(-1), block_lengths.reshape(-1), half, head_rows
    )
    taken = pass_on(given, CORE_SWAP)
    summed = add_terms(kept[:, :BLK], taken).astype(jnp.bfloat16)
    grad_rows = jnp.concatenate([summed, kept[:, BLK:]], axis=1)
    returned = lax.all_to_all(grad_rows, "ctx", split_axis=0, concat_axis=0, tiled=True)
    query_grad, key_grad, value_grad = unpack_rows(returned)
    return (query_grad[None], key_grad[None], value_grad[None], gate_grad, up_grad, down_grad)


def solution(mesh):
    in_specs = (
        P("dp", "ctx", None),
        P("dp", "ctx", None),
        P("dp", "ctx", None),
        P("dp", None, None),
        P("dp", None),
        P(),
        P("dp", "ctx", None),
        P("dp", "ctx", None),
        P("dp", "ctx", None),
        P("dp", "ctx", None),
        P("ctx", None, None),
        P("ctx", None, None),
        P("ctx", None, None),
    )
    out_specs = (
        P("dp", "ctx", None),
        P("dp", "ctx", None),
        P("dp", "ctx", None),
        P("ctx", "dp", None),
        P("ctx", "dp", None),
        P("ctx", "dp", None),
    )
    return jax.shard_map(
        per_device, mesh=mesh, in_specs=in_specs, out_specs=out_specs, check_vma=False
    )
```
